256 devices in a mesh: site: 4 (over x), fsdp: 64 (over z, y, core).
Axes of the slice: x: 4, y: 4, z: 8, core: 2. Of those that a mesh axis runs over, the one named last changes fastest.
Arguments:
- held_input: bfloat16 [4, 32768, 1536], P('site', 'fsdp'), may hold values from -16 to 16
- held_cotangent: bfloat16 [4, 32768, 1536], P('site', 'fsdp'), may hold values from -6 to 6
- proj_weight: bfloat16 [1536, 1536], P('fsdp'), may hold values from -0.15625 to 0.15625
- stem_weight: bfloat16 [3, 512, 1536], P(None, 'fsdp'), may hold values from -0.15625 to 0.15625
- seg_counts: int32 [4, 64], P('site'), may hold values from 1 to 128, 4096 in all within a row
Outputs:
- stem_grad: bfloat16 [4, 131072, 512], P('site', 'fsdp')
- weight_grad: float32 [1536, 1536], P('fsdp')
The draws below stay inside these ranges and needn't reach their ends.
Inputs may be any that keep to these rules, and one draw needn't show every extreme that they name: `seg_counts`: in every group the 64 counts sum to 4096, so that every holder slot is used; one owner has exactly 128, and a holder keeps at most 2 segments of one owner, a bound reached in every draw.
All inputs are finite; a program needn't handle non-finite values.
Results may differ from the reference program's by a relative error of at most 0.0049.
Values may be sent and summed in bfloat16 or wider, within the bound.
A program may use at most 128 MiB of HBM per device.

```python
import math
import jax
import jax.numpy as jnp
import numpy as np
from jax import lax

D = 1536
CS = 512
SEG = 8
HOLD = 64
OWN_SEG = 128
N_SITE = 4
N_FSDP = 64


def with_spikes(values, key, source, target, shards_of, factor):
    def block_of(position):
        return (jnp.arange(values.shape[position]) // (values.shape[position] // shards_of)).reshape((-1,) + (1,) * (values.ndim - 1 - position))

    near = jax.random.permutation(key, shards_of)[block_of(target)]
    second = (block_of(target) + shards_of // 2) % shards_of
    return jnp.where((block_of(source) == near) | (block_of(source) == second), factor * values, values)


def block_levels(own_key, extent, pieces, smallest, high):
    gain = 1.0
    for position, parts in pieces:
        draws = jax.random.uniform(jax.random.fold_in(jax.random.fold_in(own_key, 6), position), (parts,), jnp.float32, smallest / len(pieces), high / len(pieces))
        gain = gain * jnp.repeat(jnp.exp(draws), extent[position] // parts).reshape((-1,) + (1,) * (len(extent) - 1 - position))
    return gain


def length_profile(amount, total, bound, lean):
    weights = [(1 << 20) // math.isqrt(rank ** lean) + 1 for rank in range(2, amount + 1)]
    surplus, holding = total - bound - (amount - 1), [1] * (amount - 1)
    while surplus > 0:
        candidates = [i for i in range(amount - 1) if holding[i] < bound]
        mass, budget = sum([weights[i] for i in candidates]), surplus
        for i in candidates:
            more = min(bound - holding[i], max(1, budget * weights[i] // mass), surplus)
            holding[i] = holding[i] + more
            surplus = surplus - more
    return np.array([bound] + holding)


def uneven_parts(rng, count, total, limit, lean):
    if count == 2:
        one = jax.random.randint(rng, (), max(1, total - limit), min(limit, total - 1) + 1)
        return jnp.stack([one, total - one])
    sizes = jnp.asarray(length_profile(count, total, limit, lean), jnp.int32)
    couples = (count - 1) // 2
    donor, sink = sizes[1:1 + 2 * couples:2], sizes[2:2 + 2 * couples:2]
    slack = jnp.minimum(donor - 1, limit - sink)
    moved = jax.random.randint(jax.random.fold_in(rng, 1), (couples,), 0, 1 << 20) % (slack + 1)
    sizes = sizes.at[1:1 + 2 * couples:2].set(donor - moved).at[2:2 + 2 * couples:2].set(sink + moved)
    return sizes[jax.random.permutation(jax.random.fold_in(rng, 2), count)]


def gaussian(rng, extent, spread, bound, split=(), held_as=jnp.bfloat16):
    loudness = block_levels(rng, extent, split, -0.22, 0.18) if split else 1.0
    result = jax.random.normal(rng, extent, jnp.float32) * spread * loudness
    return jnp.minimum(jnp.maximum(result, -bound), bound).astype(held_as)


def heavy_noise(stream_key, dims, spread, bound, shards, heavy, kind=jnp.bfloat16):
    entries = spread * jax.random.normal(stream_key, dims, jnp.float32)
    if shards:
        entries = entries * block_levels(stream_key, dims, shards, -0.22, 0.18)
    return jnp.clip(with_spikes(entries, jax.random.fold_in(stream_key, 3), *heavy), -bound, bound).astype(kind)


def setup_inputs(seed: int = 0) -> dict:
    key_list = jax.random.split(jax.random.key(seed), 6)
    held_input = heavy_noise(key_list[0], (N_SITE, N_FSDP * HOLD * SEG, D), 1.0, 16.0, ((0, 4), (1, 64)), (1, 2, 64, 4.0))
    held_cotangent = gaussian(key_list[1], (N_SITE, N_FSDP * HOLD * SEG, D), 1.0, 6.0, ((0, 4), (1, 64)))
    proj_weight = gaussian(key_list[2], (D, D), D ** -0.5, 0.15625, ((0, 64),))
    stem_weight = gaussian(key_list[3], (3, CS, D), (3 * CS) ** -0.5, 0.15625, ((1, 64),))
    seg_counts = jax.vmap(lambda own: uneven_parts(own, N_FSDP, N_FSDP * HOLD, OWN_SEG, 2))(jax.random.split(key_list[4], N_SITE)).reshape((N_SITE, N_FSDP)).astype(jnp.int32)
    return dict(held_input=held_input, held_cotangent=held_cotangent, proj_weight=proj_weight, stem_weight=stem_weight, seg_counts=seg_counts)


EPSILON = 1e-05

def owner_grad_rows(input_grad, counts):
    group_size = N_FSDP
    starts = jnp.cumsum(counts) - counts
    segment = jnp.arange(OWN_SEG, dtype=jnp.int32)
    item_index = starts[:, None] + segment[None, :]
    is_live = segment[None, :] < counts[:, None]
    holder = item_index // 2 % group_size
    slot_ids = 2 * (item_index // (2 * group_size)) + item_index % 2
    row_index = jnp.where(is_live, holder * HOLD + slot_ids, 0).astype(jnp.int32)
    blocks_all = input_grad.reshape(group_size * HOLD, SEG, D)
    picked = jnp.take(blocks_all, row_index.reshape(-1), axis=0).reshape(group_size, OWN_SEG * SEG, D)
    mask_rows = jnp.repeat(is_live, SEG, axis=1)
    return jnp.where(mask_rows[:, :, None], picked, jnp.zeros((), jnp.bfloat16))

def stem_backward(frames, stem_weight):
    tap_terms = [jnp.dot(frames, stem_weight[tap_id].T, preferred_element_type=jnp.float32) for tap_id in range(3)]
    shifted = jnp.concatenate([tap_terms[0][1:], jnp.zeros((1, CS), jnp.float32)], 0)
    odd_rows = tap_terms[2] + shifted
    return jnp.stack([tap_terms[1], odd_rows], 1).reshape(2 * frames.shape[0], CS).astype(jnp.bfloat16)

def reference(held_input, held_cotangent, proj_weight, stem_weight, seg_counts):
    grad_total = jnp.zeros((D, D), jnp.float32)
    stem_list = []
    for group_id in range(N_SITE):
        inputs = held_input[group_id].astype(jnp.float32)
        cotangent = held_cotangent[group_id]
        row_mean = lax.optimization_barrier(jnp.mean(inputs, axis=-1, keepdims=True))
        centered = inputs - row_mean
        variance = lax.optimization_barrier(jnp.mean(centered * centered, axis=-1, keepdims=True))
        inverse = lax.rsqrt(variance + EPSILON)
        normed = centered * inverse
        normed_bf = normed.astype(jnp.bfloat16)
        grad_total = grad_total + jnp.dot(normed_bf.T, cotangent, preferred_element_type=jnp.float32)
        proj_back = jnp.dot(cotangent, proj_weight.T, preferred_element_type=jnp.float32)
        input_grad = cotangent.astype(jnp.float32) + inverse * (proj_back - lax.optimization_barrier(jnp.mean(proj_back, axis=-1, keepdims=True)) - normed * lax.optimization_barrier(jnp.mean(proj_back * normed, axis=-1, keepdims=True)))
        input_grad = input_grad.astype(jnp.bfloat16)
        owner_frames = owner_grad_rows(input_grad, seg_counts[group_id])
        stems = lax.map(lambda frames: stem_backward(frames, stem_weight), owner_frames)
        stem_list.append(stems.reshape(N_FSDP * 2 * OWN_SEG * SEG, CS))
    stem_grad = jnp.stack(stem_list, 0)
    weight_grad = grad_total / math.sqrt(N_SITE * N_FSDP * HOLD * SEG)
    return (stem_grad, weight_grad)
```

```python
import math

import jax
import jax.numpy as jnp
from jax import lax
from jax.sharding import PartitionSpec as P

D = 1536
SEG = 8
HOLD = 64
OWN_SEG = 128


EPSILON = 1e-05


def stem_taps(frames, stem_gathered):
    taps = jnp.einsum(
        "rd,fkcd->krfc", frames, stem_gathered, preferred_element_type=jnp.float32
    )
    return taps.reshape(taps.shape[0], taps.shape[1], -1)


def body(held_input, held_cotangent, proj_weight, stem_weight, seg_counts):
    group_size = lax.axis_size("fsdp")
    capacity = 2 * ((OWN_SEG + 2 * group_size - 1) // (2 * group_size))
    my_index = lax.axis_index("fsdp")
    inputs = held_input[0].astype(jnp.float32)
    cotangent = held_cotangent[0]
    row_mean = jnp.mean(inputs, axis=-1, keepdims=True)
    centered = inputs - row_mean
    variance = jnp.mean(centered * centered, axis=-1, keepdims=True)
    inverse = lax.rsqrt(variance + EPSILON)
    normed = centered * inverse
    normed_bf = normed.astype(jnp.bfloat16)
    rows_w = proj_weight.shape[0]
    taps_n, chans = stem_weight.shape[0], stem_weight.shape[1]
    joined = jnp.concatenate([proj_weight, stem_weight.reshape(taps_n * chans, D)], 0)
    gathered = lax.all_gather(joined, "fsdp", axis=0, tiled=False)
    full_weight = gathered[:, :rows_w].reshape(group_size * rows_w, D)
    stem_gathered = gathered[:, rows_w:].reshape(group_size, taps_n, chans, D)
    proj_back = lax.dot_general(
        cotangent,
        full_weight,
        (((1,), (1,)), ((), ())),
        preferred_element_type=jnp.float32,
    )
    input_grad = cotangent.astype(jnp.float32) + inverse * (
        proj_back
        - jnp.mean(proj_back, axis=-1, keepdims=True)
        - normed * jnp.mean(proj_back * normed, axis=-1, keepdims=True)
    )
    input_grad = input_grad.astype(jnp.bfloat16)
    counts = seg_counts[0]
    endings = jnp.cumsum(counts)
    starts = endings - counts
    slot_ids = jnp.arange(HOLD, dtype=jnp.int32)
    item_index = 2 * (slot_ids // 2 * group_size + my_index) + slot_ids % 2
    owner_ids = jnp.sum((item_index[:, None] >= endings[None, :]).astype(jnp.int32), axis=1)
    earlier = (slot_ids[None, :] < slot_ids[:, None]) & (owner_ids[None, :] == owner_ids[:, None])
    rank_ids = jnp.sum(earlier.astype(jnp.int32), axis=1)
    target = owner_ids * capacity + rank_ids
    positions = jnp.arange(group_size * capacity, dtype=jnp.int32)
    matched = target[None, :] == positions[:, None]
    filled = jnp.any(matched, axis=1)
    source = jnp.sum(jnp.where(matched, slot_ids[None, :], 0), axis=1)
    owner_hit = jnp.arange(group_size, dtype=jnp.int32) == my_index
    my_count = jnp.sum(jnp.where(owner_hit, counts, 0))
    my_start = jnp.sum(jnp.where(owner_hit, starts, 0))
    segment = jnp.arange(OWN_SEG, dtype=jnp.int32)
    is_live = segment < my_count
    holder = (my_start + segment) // 2 % group_size
    before = (
        (segment[None, :] < segment[:, None])
        & (holder[None, :] == holder[:, None])
        & is_live[None, :]
    )
    holder_rank = jnp.sum(before.astype(jnp.int32), axis=1)
    row_index = jnp.where(is_live, holder * capacity + holder_rank, 0)
    held_segments = input_grad.reshape(HOLD, SEG, D)
    zero_bf = jnp.zeros((), jnp.bfloat16)
    send_rows = jnp.where(filled[:, None, None], jnp.take(held_segments, source, axis=0), zero_bf)
    received = lax.all_to_all(
        send_rows.reshape(group_size, capacity, SEG, D),
        "fsdp",
        split_axis=0,
        concat_axis=0,
        tiled=True,
    )
    picked = jnp.take(received.reshape(group_size * capacity, SEG, D), row_index, axis=0)
    frames = jnp.where(is_live[:, None, None], picked, zero_bf).reshape(OWN_SEG * SEG, D)
    tap_terms = stem_taps(frames, stem_gathered)
    shifted = jnp.concatenate(
        [tap_terms[0][1:], jnp.zeros((1, tap_terms.shape[2]), jnp.float32)], 0
    )
    odd_rows = tap_terms[2] + shifted
    stem_rows = (
        jnp.stack([tap_terms[1], odd_rows], 1)
        .reshape(2 * OWN_SEG * SEG, tap_terms.shape[2])
        .astype(jnp.bfloat16)
    )
    partial = lax.dot_general(
        normed_bf, cotangent, (((0,), (0,)), ((), ())), preferred_element_type=jnp.float32
    )
    partial, gathered = lax.optimization_barrier((partial, gathered))
    shard_sum = lax.psum_scatter(
        partial,
        "fsdp",
        scatter_dimension=0,
        tiled=True,
    )
    shard_sum = lax.psum(shard_sum, "site")
    weight_grad = shard_sum / math.sqrt(lax.axis_size("site") * group_size * HOLD * SEG)
    return (stem_rows[None], weight_grad)


def solution(mesh):
    placed = (
        P("site", "fsdp", None),
        P("site", "fsdp", None),
        P("fsdp", None),
        P(None, "fsdp", None),
        P("site", None),
    )
    return jax.shard_map(
        body,
        mesh=mesh,
        in_specs=placed,
        out_specs=(P("site", "fsdp", None), P("fsdp", None)),
        check_vma=False,
    )
```

```python
import functools
import math

import jax
import jax.numpy as jnp
from jax import lax
from jax.experimental import pallas as pl
from jax.experimental.pallas import tpu as pltpu
from jax.sharding import PartitionSpec as P

D = 1536
SEG = 8
HOLD = 64
OWN_SEG = 128


EPSILON = 1e-05


def stem_taps(frames, stem_gathered):
    taps = jnp.einsum(
        "rd,fkcd->krfc", frames, stem_gathered, preferred_element_type=jnp.float32
    )
    return taps.reshape(taps.shape[0], taps.shape[1], -1)


def site_sum_kernel(n_site, part_ref, out_ref, slots, send_sems, recv_sems):
    me = lax.axis_index("site")
    col = lax.axis_index("fsdp")
    mesh_kind = pl.DeviceIdType.MESH
    barrier = pltpu.get_barrier_semaphore()
    for step in range(1, n_site):
        peer = lax.rem(me + step, n_site)
        pl.semaphore_signal(barrier, inc=1, device_id=(peer, col), device_id_type=mesh_kind)
    pl.semaphore_wait(barrier, n_site - 1)
    copies = []
    for step in range(1, n_site):
        peer = lax.rem(me + step, n_site)
        copy = pltpu.make_async_remote_copy(
            src_ref=part_ref,
            dst_ref=slots.at[me],
            send_sem=send_sems.at[step],
            recv_sem=recv_sems.at[me],
            device_id=(peer, col),
            device_id_type=mesh_kind,
        )
        copy.start()
        copies.append(copy)
    slots[me] = part_ref[...]
    for copy in copies:
        copy.wait_send()
    for step in range(1, n_site):
        src = lax.rem(me + step, n_site)
        pltpu.make_async_remote_copy(
            src_ref=part_ref,
            dst_ref=slots.at[src],
            send_sem=send_sems.at[0],
            recv_sem=recv_sems.at[src],
            device_id=(src, col),
            device_id_type=mesh_kind,
        ).wait_recv()
    total = slots[0]
    for index in range(1, n_site):
        total = total + slots[index]
    out_ref[...] = total


def site_sum(part):
    n_site = lax.axis_size("site")
    return pl.pallas_call(
        functools.partial(site_sum_kernel, n_site),
        out_shape=jax.ShapeDtypeStruct(part.shape, part.dtype),
        in_specs=[pl.BlockSpec(memory_space=pltpu.VMEM)],
        out_specs=pl.BlockSpec(memory_space=pltpu.VMEM),
        scratch_shapes=[
            pltpu.VMEM((n_site,) + part.shape, part.dtype),
            pltpu.SemaphoreType.DMA((n_site,)),
            pltpu.SemaphoreType.DMA((n_site,)),
        ],
        compiler_params=pltpu.CompilerParams(collective_id=0, has_side_effects=True),
    )(part)


def body(held_input, held_cotangent, proj_weight, stem_weight, seg_counts):
    group_size = lax.axis_size("fsdp")
    capacity = 2 * ((OWN_SEG + 2 * group_size - 1) // (2 * group_size))
    my_index = lax.axis_index("fsdp")
    inputs = held_input[0].astype(jnp.float32)
    cotangent = held_cotangent[0]
    row_mean = jnp.mean(inputs, axis=-1, keepdims=True)
    centered = inputs - row_mean
    variance = jnp.mean(centered * centered, axis=-1, keepdims=True)
    inverse = lax.rsqrt(variance + EPSILON)
    normed = centered * inverse
    normed_bf = normed.astype(jnp.bfloat16)
    rows_w = proj_weight.shape[0]
    taps_n, chans = stem_weight.shape[0], stem_weight.shape[1]
    joined = jnp.concatenate([proj_weight, stem_weight.reshape(taps_n * chans, D)], 0)
    gathered = lax.all_gather(joined, "fsdp", axis=0, tiled=False)
    full_weight = gathered[:, :rows_w].reshape(group_size * rows_w, D)
    stem_gathered = gathered[:, rows_w:].reshape(group_size, taps_n, chans, D)
    proj_back = lax.dot_general(
        cotangent,
        full_weight,
        (((1,), (1,)), ((), ())),
        preferred_element_type=jnp.float32,
    )
    input_grad = cotangent.astype(jnp.float32) + inverse * (
        proj_back
        - jnp.mean(proj_back, axis=-1, keepdims=True)
        - normed * jnp.mean(proj_back * normed, axis=-1, keepdims=True)
    )
    input_grad = input_grad.astype(jnp.bfloat16)
    counts = seg_counts[0]
    endings = jnp.cumsum(counts)
    starts = endings - counts
    slot_ids = jnp.arange(HOLD, dtype=jnp.int32)
    item_index = 2 * (slot_ids // 2 * group_size + my_index) + slot_ids % 2
    owner_ids = jnp.sum((item_index[:, None] >= endings[None, :]).astype(jnp.int32), axis=1)
    earlier = (slot_ids[None, :] < slot_ids[:, None]) & (owner_ids[None, :] == owner_ids[:, None])
    rank_ids = jnp.sum(earlier.astype(jnp.int32), axis=1)
    target = owner_ids * capacity + rank_ids
    positions = jnp.arange(group_size * capacity, dtype=jnp.int32)
    matched = target[None, :] == positions[:, None]
    filled = jnp.any(matched, axis=1)
    source = jnp.sum(jnp.where(matched, slot_ids[None, :], 0), axis=1)
    owner_hit = jnp.arange(group_size, dtype=jnp.int32) == my_index
    my_count = jnp.sum(jnp.where(owner_hit, counts, 0))
    my_start = jnp.sum(jnp.where(owner_hit, starts, 0))
    segment = jnp.arange(OWN_SEG, dtype=jnp.int32)
    is_live = segment < my_count
    holder = (my_start + segment) // 2 % group_size
    before = (
        (segment[None, :] < segment[:, None])
        & (holder[None, :] == holder[:, None])
        & is_live[None, :]
    )
    holder_rank = jnp.sum(before.astype(jnp.int32), axis=1)
    row_index = jnp.where(is_live, holder * capacity + holder_rank, 0)
    held_segments = input_grad.reshape(HOLD, SEG, D)
    zero_bf = jnp.zeros((), jnp.bfloat16)
    send_rows = jnp.where(filled[:, None, None], jnp.take(held_segments, source, axis=0), zero_bf)
    received = lax.all_to_all(
        send_rows.reshape(group_size, capacity, SEG, D),
        "fsdp",
        split_axis=0,
        concat_axis=0,
        tiled=True,
    )
    picked = jnp.take(received.reshape(group_size * capacity, SEG, D), row_index, axis=0)
    frames = jnp.where(is_live[:, None, None], picked, zero_bf).reshape(OWN_SEG * SEG, D)
    tap_terms = stem_taps(frames, stem_gathered)
    shifted = jnp.concatenate(
        [tap_terms[0][1:], jnp.zeros((1, tap_terms.shape[2]), jnp.float32)], 0
    )
    odd_rows = tap_terms[2] + shifted
    stem_rows = (
        jnp.stack([tap_terms[1], odd_rows], 1)
        .reshape(2 * OWN_SEG * SEG, tap_terms.shape[2])
        .astype(jnp.bfloat16)
    )
    partial = lax.dot_general(
        normed_bf, cotangent, (((0,), (0,)), ((), ())), preferred_element_type=jnp.float32
    )
    partial, gathered = lax.optimization_barrier((partial, gathered))
    shard_sum = lax.psum_scatter(
        partial,
        "fsdp",
        scatter_dimension=0,
        tiled=True,
    )
    shard_sum = site_sum(shard_sum)
    weight_grad = shard_sum / math.sqrt(lax.axis_size("site") * group_size * HOLD * SEG)
    return (stem_rows[None], weight_grad)


def solution(mesh):
    placed = (
        P("site", "fsdp", None),
        P("site", "fsdp", None),
        P("fsdp", None),
        P(None, "fsdp", None),
        P("site", None),
    )
    return jax.shard_map(
        body,
        mesh=mesh,
        in_specs=placed,
        out_specs=(P("site", "fsdp", None), P("fsdp", None)),
        check_vma=False,
    )
```

```python
import functools
import math

import jax
import jax.numpy as jnp
from jax import lax
from jax.experimental import pallas as pl
from jax.experimental.pallas import tpu as pltpu
from jax.sharding import PartitionSpec as P

D = 1536
SEG = 8
HOLD = 64
OWN_SEG = 128


EPSILON = 1e-05


def stem_taps(frames, stem_gathered):
    taps = jnp.einsum(
        "rd,fkcd->krfc", frames, stem_gathered, preferred_element_type=jnp.float32
    )
    return taps.reshape(taps.shape[0], taps.shape[1], -1)


def site_sum_kernel(n_site, part_ref, out_ref, slots, send_sems, recv_sems):
    me = lax.axis_index("site")
    col = lax.axis_index("fsdp")
    mesh_kind = pl.DeviceIdType.MESH
    barrier = pltpu.get_barrier_semaphore()
    for step in range(1, n_site):
        peer = lax.rem(me + step, n_site)
        pl.semaphore_signal(barrier, inc=1, device_id=(peer, col), device_id_type=mesh_kind)
    pl.semaphore_wait(barrier, n_site - 1)
    copies = []
    for step in range(1, n_site):
        peer = lax.rem(me + step, n_site)
        copy = pltpu.make_async_remote_copy(
            src_ref=part_ref,
            dst_ref=slots.at[me],
            send_sem=send_sems.at[step],
            recv_sem=recv_sems.at[me],
            device_id=(peer, col),
            device_id_type=mesh_kind,
        )
        copy.start()
        copies.append(copy)
    slots[me] = part_ref[...]
    for copy in copies:
        copy.wait_send()
    for step in range(1, n_site):
        src = lax.rem(me + step, n_site)
        pltpu.make_async_remote_copy(
            src_ref=part_ref,
            dst_ref=slots.at[src],
            send_sem=send_sems.at[0],
            recv_sem=recv_sems.at[src],
            device_id=(src, col),
            device_id_type=mesh_kind,
        ).wait_recv()
    total = slots[0]
    for index in range(1, n_site):
        total = total + slots[index]
    out_ref[...] = total


def fsdp_sum_kernel(n_chip, part_ref, out_ref, xbuf, rbuf, sems0, send_sems, recv_sems):
    me = lax.axis_index("fsdp")
    site = lax.axis_index("site")
    core = lax.rem(me, 2)
    chip = me // 2
    sibling = me + 1 - 2 * core
    mesh_kind = pl.DeviceIdType.MESH
    barrier = pltpu.get_barrier_semaphore()
    pl.semaphore_signal(barrier, inc=1, device_id=(site, sibling), device_id_type=mesh_kind)

    def greet(step, carry):
        peer = 2 * lax.rem(chip + step, n_chip) + core
        pl.semaphore_signal(barrier, inc=1, device_id=(site, peer), device_id_type=mesh_kind)
        return carry

    lax.fori_loop(1, n_chip, greet, 0)
    pl.semaphore_wait(barrier, n_chip)
    swap = pltpu.make_async_remote_copy(
        src_ref=part_ref.at[1 - core],
        dst_ref=xbuf,
        send_sem=sems0.at[0],
        recv_sem=sems0.at[1],
        device_id=(site, sibling),
        device_id_type=mesh_kind,
    )
    swap.start()
    swap.wait()

    def push(step, carry):
        target = lax.rem(chip + step, n_chip)
        xbuf[target] = xbuf[target] + part_ref[core, target]
        pltpu.make_async_remote_copy(
            src_ref=xbuf.at[target],
            dst_ref=rbuf.at[chip],
            send_sem=send_sems.at[target],
            recv_sem=recv_sems.at[chip],
            device_id=(site, 2 * target + core),
            device_id_type=mesh_kind,
        ).start()
        return carry

    lax.fori_loop(1, n_chip, push, 0)
    rbuf[chip] = xbuf[chip] + part_ref[core, chip]

    def drain(step, carry):
        target = lax.rem(chip + step, n_chip)
        pltpu.make_async_remote_copy(
            src_ref=xbuf.at[target],
            dst_ref=rbuf.at[chip],
            send_sem=send_sems.at[target],
            recv_sem=recv_sems.at[chip],
            device_id=(site, 2 * target + core),
            device_id_type=mesh_kind,
        ).wait_send()
        pltpu.make_async_remote_copy(
            src_ref=xbuf.at[target],
            dst_ref=rbuf.at[target],
            send_sem=send_sems.at[target],
            recv_sem=recv_sems.at[target],
            device_id=(site, 2 * target + core),
            device_id_type=mesh_kind,
        ).wait_recv()
        return carry

    lax.fori_loop(1, n_chip, drain, 0)
    out_ref[...] = rbuf[0]

    def gather_sum(index, carry):
        out_ref[...] = out_ref[...] + rbuf[index]
        return carry

    lax.fori_loop(1, n_chip, gather_sum, 0)


def fsdp_sum(part):
    n_chip = part.shape[1]
    block = part.shape[2:]
    return pl.pallas_call(
        functools.partial(fsdp_sum_kernel, n_chip),
        out_shape=jax.ShapeDtypeStruct(block, part.dtype),
        in_specs=[pl.BlockSpec(memory_space=pltpu.VMEM)],
        out_specs=pl.BlockSpec(memory_space=pltpu.VMEM),
        scratch_shapes=[
            pltpu.VMEM((n_chip,) + block, part.dtype),
            pltpu.VMEM((n_chip,) + block, part.dtype),
            pltpu.SemaphoreType.DMA((2,)),
            pltpu.SemaphoreType.DMA((n_chip,)),
            pltpu.SemaphoreType.DMA((n_chip,)),
        ],
        compiler_params=pltpu.CompilerParams(collective_id=1, has_side_effects=True),
    )(part)


def site_sum(part):
    n_site = lax.axis_size("site")
    return pl.pallas_call(
        functools.partial(site_sum_kernel, n_site),
        out_shape=jax.ShapeDtypeStruct(part.shape, part.dtype),
        in_specs=[pl.BlockSpec(memory_space=pltpu.VMEM)],
        out_specs=pl.BlockSpec(memory_space=pltpu.VMEM),
        scratch_shapes=[
            pltpu.VMEM((n_site,) + part.shape, part.dtype),
            pltpu.SemaphoreType.DMA((n_site,)),
            pltpu.SemaphoreType.DMA((n_site,)),
        ],
        compiler_params=pltpu.CompilerParams(collective_id=0, has_side_effects=True),
    )(part)


def body(held_input, held_cotangent, proj_weight, stem_weight, seg_counts):
    group_size = lax.axis_size("fsdp")
    capacity = 2 * ((OWN_SEG + 2 * group_size - 1) // (2 * group_size))
    my_index = lax.axis_index("fsdp")
    inputs = held_input[0].astype(jnp.float32)
    cotangent = held_cotangent[0]
    row_mean = jnp.mean(inputs, axis=-1, keepdims=True)
    centered = inputs - row_mean
    variance = jnp.mean(centered * centered, axis=-1, keepdims=True)
    inverse = lax.rsqrt(variance + EPSILON)
    normed = centered * inverse
    normed_bf = normed.astype(jnp.bfloat16)
    rows_w = proj_weight.shape[0]
    taps_n, chans = stem_weight.shape[0], stem_weight.shape[1]
    joined = jnp.concatenate([proj_weight, stem_weight.reshape(taps_n * chans, D)], 0)
    gathered = lax.all_gather(joined, "fsdp", axis=0, tiled=False)
    full_weight = gathered[:, :rows_w].reshape(group_size * rows_w, D)
    stem_gathered = gathered[:, rows_w:].reshape(group_size, taps_n, chans, D)
    proj_back = lax.dot_general(
        cotangent,
        full_weight,
        (((1,), (1,)), ((), ())),
        preferred_element_type=jnp.float32,
    )
    input_grad = cotangent.astype(jnp.float32) + inverse * (
        proj_back
        - jnp.mean(proj_back, axis=-1, keepdims=True)
        - normed * jnp.mean(proj_back * normed, axis=-1, keepdims=True)
    )
    input_grad = input_grad.astype(jnp.bfloat16)
    counts = seg_counts[0]
    endings = jnp.cumsum(counts)
    starts = endings - counts
    slot_ids = jnp.arange(HOLD, dtype=jnp.int32)
    item_index = 2 * (slot_ids // 2 * group_size + my_index) + slot_ids % 2
    owner_ids = jnp.sum((item_index[:, None] >= endings[None, :]).astype(jnp.int32), axis=1)
    earlier = (slot_ids[None, :] < slot_ids[:, None]) & (owner_ids[None, :] == owner_ids[:, None])
    rank_ids = jnp.sum(earlier.astype(jnp.int32), axis=1)
    target = owner_ids * capacity + rank_ids
    positions = jnp.arange(group_size * capacity, dtype=jnp.int32)
    matched = target[None, :] == positions[:, None]
    filled = jnp.any(matched, axis=1)
    source = jnp.sum(jnp.where(matched, slot_ids[None, :], 0), axis=1)
    owner_hit = jnp.arange(group_size, dtype=jnp.int32) == my_index
    my_count = jnp.sum(jnp.where(owner_hit, counts, 0))
    my_start = jnp.sum(jnp.where(owner_hit, starts, 0))
    segment = jnp.arange(OWN_SEG, dtype=jnp.int32)
    is_live = segment < my_count
    holder = (my_start + segment) // 2 % group_size
    before = (
        (segment[None, :] < segment[:, None])
        & (holder[None, :] == holder[:, None])
        & is_live[None, :]
    )
    holder_rank = jnp.sum(before.astype(jnp.int32), axis=1)
    row_index = jnp.where(is_live, holder * capacity + holder_rank, 0)
    held_segments = input_grad.reshape(HOLD, SEG, D)
    zero_bf = jnp.zeros((), jnp.bfloat16)
    send_rows = jnp.where(filled[:, None, None], jnp.take(held_segments, source, axis=0), zero_bf)
    received = lax.all_to_all(
        send_rows.reshape(group_size, capacity, SEG, D),
        "fsdp",
        split_axis=0,
        concat_axis=0,
        tiled=True,
    )
    picked = jnp.take(received.reshape(group_size * capacity, SEG, D), row_index, axis=0)
    frames = jnp.where(is_live[:, None, None], picked, zero_bf).reshape(OWN_SEG * SEG, D)
    tap_terms = stem_taps(frames, stem_gathered)
    shifted = jnp.concatenate(
        [tap_terms[0][1:], jnp.zeros((1, tap_terms.shape[2]), jnp.float32)], 0
    )
    odd_rows = tap_terms[2] + shifted
    stem_rows = (
        jnp.stack([tap_terms[1], odd_rows], 1)
        .reshape(2 * OWN_SEG * SEG, tap_terms.shape[2])
        .astype(jnp.bfloat16)
    )
    rows_out = D // group_size
    partial = jnp.einsum(
        "rckj,rd->kcjd",
        normed_bf.reshape(normed_bf.shape[0], group_size // 2, 2, rows_out),
        cotangent,
        preferred_element_type=jnp.float32,
    )
    shard_sum = fsdp_sum(partial)
    shard_sum = site_sum(shard_sum)
    weight_grad = shard_sum / math.sqrt(lax.axis_size("site") * group_size * HOLD * SEG)
    return (stem_rows[None], weight_grad)


def solution(mesh):
    placed = (
        P("site", "fsdp", None),
        P("site", "fsdp", None),
        P("fsdp", None),
        P(None, "fsdp", None),
        P("site", None),
    )
    return jax.shard_map(
        body,
        mesh=mesh,
        in_specs=placed,
        out_specs=(P("site", "fsdp", None), P("fsdp", None)),
        check_vma=False,
    )
```

```python
import functools
import math

import jax
import jax.numpy as jnp
from jax import lax
from jax.experimental import pallas as pl
from jax.experimental.pallas import tpu as pltpu
from jax.sharding import PartitionSpec as P

D = 1536
SEG = 8
HOLD = 64
OWN_SEG = 128


EPSILON = 1e-05


def stem_taps(frames, stem_gathered):
    taps = jnp.einsum(
        "rd,fkcd->krfc", frames, stem_gathered, preferred_element_type=jnp.float32
    )
    return taps.reshape(taps.shape[0], taps.shape[1], -1)


def site_sum_kernel(n_site, part_ref, out_ref, slots, send_sems, recv_sems):
    me = lax.axis_index("site")
    col = lax.axis_index("fsdp")
    mesh_kind = pl.DeviceIdType.MESH
    barrier = pltpu.get_barrier_semaphore()
    for step in range(1, n_site):
        peer = lax.rem(me + step, n_site)
        pl.semaphore_signal(barrier, inc=1, device_id=(peer, col), device_id_type=mesh_kind)
    pl.semaphore_wait(barrier, n_site - 1)
    copies = []
    for step in range(1, n_site):
        peer = lax.rem(me + step, n_site)
        copy = pltpu.make_async_remote_copy(
            src_ref=part_ref,
            dst_ref=slots.at[me],
            send_sem=send_sems.at[step],
            recv_sem=recv_sems.at[me],
            device_id=(peer, col),
            device_id_type=mesh_kind,
        )
        copy.start()
        copies.append(copy)
    slots[me] = part_ref[...]
    for copy in copies:
        copy.wait_send()
    for step in range(1, n_site):
        src = lax.rem(me + step, n_site)
        pltpu.make_async_remote_copy(
            src_ref=part_ref,
            dst_ref=slots.at[src],
            send_sem=send_sems.at[0],
            recv_sem=recv_sems.at[src],
            device_id=(src, col),
            device_id_type=mesh_kind,
        ).wait_recv()
    total = slots[0]
    for index in range(1, n_site):
        total = total + slots[index]
    out_ref[...] = total


def fsdp_sum_kernel(n_chip, part_ref, out_ref, xbuf, rbuf, sems0, send_sems, recv_sems):
    me = lax.axis_index("fsdp")
    site = lax.axis_index("site")
    core = lax.rem(me, 2)
    chip = me // 2
    sibling = me + 1 - 2 * core
    mesh_kind = pl.DeviceIdType.MESH
    barrier = pltpu.get_barrier_semaphore()
    pl.semaphore_signal(barrier, inc=1, device_id=(site, sibling), device_id_type=mesh_kind)

    def greet(step, carry):
        peer = 2 * lax.rem(chip + step, n_chip) + core
        pl.semaphore_signal(barrier, inc=1, device_id=(site, peer), device_id_type=mesh_kind)
        return carry

    lax.fori_loop(1, n_chip, greet, 0)
    pl.semaphore_wait(barrier, n_chip)
    swap = pltpu.make_async_remote_copy(
        src_ref=part_ref.at[1 - core],
        dst_ref=xbuf,
        send_sem=sems0.at[0],
        recv_sem=sems0.at[1],
        device_id=(site, sibling),
        device_id_type=mesh_kind,
    )
    swap.start()
    swap.wait()

    def push(step, carry):
        target = lax.rem(chip + step, n_chip)
        xbuf[target] = xbuf[target] + part_ref[core, target]
        pltpu.make_async_remote_copy(
            src_ref=xbuf.at[target],
            dst_ref=rbuf.at[chip],
            send_sem=send_sems.at[target],
            recv_sem=recv_sems.at[chip],
            device_id=(site, 2 * target + core),
            device_id_type=mesh_kind,
        ).start()
        return carry

    lax.fori_loop(1, n_chip, push, 0)
    rbuf[chip] = xbuf[chip] + part_ref[core, chip]

    def drain(step, carry):
        target = lax.rem(chip + step, n_chip)
        pltpu.make_async_remote_copy(
            src_ref=xbuf.at[target],
            dst_ref=rbuf.at[chip],
            send_sem=send_sems.at[target],
            recv_sem=recv_sems.at[chip],
            device_id=(site, 2 * target + core),
            device_id_type=mesh_kind,
        ).wait_send()
        pltpu.make_async_remote_copy(
            src_ref=xbuf.at[target],
            dst_ref=rbuf.at[target],
            send_sem=send_sems.at[target],
            recv_sem=recv_sems.at[target],
            device_id=(site, 2 * target + core),
            device_id_type=mesh_kind,
        ).wait_recv()
        return carry

    lax.fori_loop(1, n_chip, drain, 0)
    out_ref[...] = rbuf[0]

    def gather_sum(index, carry):
        out_ref[...] = out_ref[...] + rbuf[index]
        return carry

    lax.fori_loop(1, n_chip, gather_sum, 0)


def fsdp_sum(part):
    n_chip = part.shape[1]
    block = part.shape[2:]
    return pl.pallas_call(
        functools.partial(fsdp_sum_kernel, n_chip),
        out_shape=jax.ShapeDtypeStruct(block, part.dtype),
        in_specs=[pl.BlockSpec(memory_space=pltpu.VMEM)],
        out_specs=pl.BlockSpec(memory_space=pltpu.VMEM),
        scratch_shapes=[
            pltpu.VMEM((n_chip,) + block, part.dtype),
            pltpu.VMEM((n_chip,) + block, part.dtype),
            pltpu.SemaphoreType.DMA((2,)),
            pltpu.SemaphoreType.DMA((n_chip,)),
            pltpu.SemaphoreType.DMA((n_chip,)),
        ],
        compiler_params=pltpu.CompilerParams(collective_id=1, has_side_effects=True),
    )(part)


def site_sum(part):
    n_site = lax.axis_size("site")
    return pl.pallas_call(
        functools.partial(site_sum_kernel, n_site),
        out_shape=jax.ShapeDtypeStruct(part.shape, part.dtype),
        in_specs=[pl.BlockSpec(memory_space=pltpu.VMEM)],
        out_specs=pl.BlockSpec(memory_space=pltpu.VMEM),
        scratch_shapes=[
            pltpu.VMEM((n_site,) + part.shape, part.dtype),
            pltpu.SemaphoreType.DMA((n_site,)),
            pltpu.SemaphoreType.DMA((n_site,)),
        ],
        compiler_params=pltpu.CompilerParams(collective_id=0, has_side_effects=True),
    )(part)


def body(held_input, held_cotangent, proj_weight, stem_weight, seg_counts):
    group_size = lax.axis_size("fsdp")
    capacity = 2 * ((OWN_SEG + 2 * group_size - 1) // (2 * group_size))
    my_index = lax.axis_index("fsdp")
    inputs = held_input[0].astype(jnp.float32)
    cotangent = held_cotangent[0]
    row_mean = jnp.mean(inputs, axis=-1, keepdims=True)
    centered = inputs - row_mean
    variance = jnp.mean(centered * centered, axis=-1, keepdims=True)
    inverse = lax.rsqrt(variance + EPSILON)
    normed = centered * inverse
    normed_bf = normed.astype(jnp.bfloat16)
    rows_w = proj_weight.shape[0]
    taps_n, chans = stem_weight.shape[0], stem_weight.shape[1]
    joined = jnp.concatenate([proj_weight, stem_weight.reshape(taps_n * chans, D)], 0)
    gathered = lax.all_gather(joined, "fsdp", axis=0, tiled=False)
    rows_out = D // group_size
    half = D // 2
    partial = jnp.einsum(
        "rckj,rd->kcjd",
        normed_bf.reshape(normed_bf.shape[0], group_size // 2, 2, rows_out),
        cotangent[:, :half],
        preferred_element_type=jnp.float32,
    )
    kernel_sum = fsdp_sum(partial)
    partial_sc = lax.dot_general(
        normed_bf, cotangent[:, half:], (((0,), (0,)), ((), ())), preferred_element_type=jnp.float32
    )
    partial_sc, kernel_sum, gathered = lax.optimization_barrier((partial_sc, kernel_sum, gathered))
    queue_sum = lax.psum_scatter(partial_sc, "fsdp", scatter_dimension=0, tiled=True)
    shard_sum = jnp.concatenate([kernel_sum, queue_sum], 1)
    full_weight = gathered[:, :rows_w].reshape(group_size * rows_w, D)
    stem_gathered = gathered[:, rows_w:].reshape(group_size, taps_n, chans, D)
    proj_back = lax.dot_general(
        cotangent,
        full_weight,
        (((1,), (1,)), ((), ())),
        preferred_element_type=jnp.float32,
    )
    input_grad = cotangent.astype(jnp.float32) + inverse * (
        proj_back
        - jnp.mean(proj_back, axis=-1, keepdims=True)
        - normed * jnp.mean(proj_back * normed, axis=-1, keepdims=True)
    )
    input_grad = input_grad.astype(jnp.bfloat16)
    counts = seg_counts[0]
    endings = jnp.cumsum(counts)
    starts = endings - counts
    slot_ids = jnp.arange(HOLD, dtype=jnp.int32)
    item_index = 2 * (slot_ids // 2 * group_size + my_index) + slot_ids % 2
    owner_ids = jnp.sum((item_index[:, None] >= endings[None, :]).astype(jnp.int32), axis=1)
    earlier = (slot_ids[None, :] < slot_ids[:, None]) & (owner_ids[None, :] == owner_ids[:, None])
    rank_ids = jnp.sum(earlier.astype(jnp.int32), axis=1)
    target = owner_ids * capacity + rank_ids
    positions = jnp.arange(group_size * capacity, dtype=jnp.int32)
    matched = target[None, :] == positions[:, None]
    filled = jnp.any(matched, axis=1)
    source = jnp.sum(jnp.where(matched, slot_ids[None, :], 0), axis=1)
    owner_hit = jnp.arange(group_size, dtype=jnp.int32) == my_index
    my_count = jnp.sum(jnp.where(owner_hit, counts, 0))
    my_start = jnp.sum(jnp.where(owner_hit, starts, 0))
    segment = jnp.arange(OWN_SEG, dtype=jnp.int32)
    is_live = segment < my_count
    holder = (my_start + segment) // 2 % group_size
    before = (
        (segment[None, :] < segment[:, None])
        & (holder[None, :] == holder[:, None])
        & is_live[None, :]
    )
    holder_rank = jnp.sum(before.astype(jnp.int32), axis=1)
    row_index = jnp.where(is_live, holder * capacity + holder_rank, 0)
    held_segments = input_grad.reshape(HOLD, SEG, D)
    zero_bf = jnp.zeros((), jnp.bfloat16)
    send_rows = jnp.where(filled[:, None, None], jnp.take(held_segments, source, axis=0), zero_bf)
    received = lax.all_to_all(
        send_rows.reshape(group_size, capacity, SEG, D),
        "fsdp",
        split_axis=0,
        concat_axis=0,
        tiled=True,
    )
    picked = jnp.take(received.reshape(group_size * capacity, SEG, D), row_index, axis=0)
    frames = jnp.where(is_live[:, None, None], picked, zero_bf).reshape(OWN_SEG * SEG, D)
    tap_terms = stem_taps(frames, stem_gathered)
    shifted = jnp.concatenate(
        [tap_terms[0][1:], jnp.zeros((1, tap_terms.shape[2]), jnp.float32)], 0
    )
    odd_rows = tap_terms[2] + shifted
    stem_rows = (
        jnp.stack([tap_terms[1], odd_rows], 1)
        .reshape(2 * OWN_SEG * SEG, tap_terms.shape[2])
        .astype(jnp.bfloat16)
    )
    shard_sum = site_sum(shard_sum)
    weight_grad = shard_sum / math.sqrt(lax.axis_size("site") * group_size * HOLD * SEG)
    return (stem_rows[None], weight_grad)


def solution(mesh):
    placed = (
        P("site", "fsdp", None),
        P("site", "fsdp", None),
        P("fsdp", None),
        P(None, "fsdp", None),
        P("site", None),
    )
    return jax.shard_map(
        body,
        mesh=mesh,
        in_specs=placed,
        out_specs=(P("site", "fsdp", None), P("fsdp", None)),
        check_vma=False,
    )
```

```python
import functools
import math

import jax
import jax.numpy as jnp
from jax import lax
from jax.experimental import pallas as pl
from jax.experimental.pallas import tpu as pltpu
from jax.sharding import PartitionSpec as P

D = 1536
SEG = 8
HOLD = 64
OWN_SEG = 128
N_Z = 8


EPSILON = 1e-05


def stem_taps(frames, stem_gathered):
    taps = jnp.einsum(
        "rd,fkcd->krfc", frames, stem_gathered, preferred_element_type=jnp.float32
    )
    return taps.reshape(taps.shape[0], taps.shape[1], -1)


def site_sum_kernel(n_site, part_ref, out_ref, slots, send_sems, recv_sems):
    me = lax.axis_index("site")
    col = lax.axis_index("fsdp")
    mesh_kind = pl.DeviceIdType.MESH
    barrier = pltpu.get_barrier_semaphore()
    for step in range(1, n_site):
        peer = lax.rem(me + step, n_site)
        pl.semaphore_signal(barrier, inc=1, device_id=(peer, col), device_id_type=mesh_kind)
    pl.semaphore_wait(barrier, n_site - 1)
    copies = []
    for step in range(1, n_site):
        peer = lax.rem(me + step, n_site)
        copy = pltpu.make_async_remote_copy(
            src_ref=part_ref,
            dst_ref=slots.at[me],
            send_sem=send_sems.at[step],
            recv_sem=recv_sems.at[me],
            device_id=(peer, col),
            device_id_type=mesh_kind,
        )
        copy.start()
        copies.append(copy)
    slots[me] = part_ref[...]
    for copy in copies:
        copy.wait_send()
    for step in range(1, n_site):
        src = lax.rem(me + step, n_site)
        pltpu.make_async_remote_copy(
            src_ref=part_ref,
            dst_ref=slots.at[src],
            send_sem=send_sems.at[0],
            recv_sem=recv_sems.at[src],
            device_id=(src, col),
            device_id_type=mesh_kind,
        ).wait_recv()
    total = slots[0]
    for index in range(1, n_site):
        total = total + slots[index]
    out_ref[...] = total


def ring_pass(n, left, right, chunk_of, land, recv_buf, send_buf, recv_sems, send_sems, free_sem):
    mesh_kind = pl.DeviceIdType.MESH
    for step in range(n):
        slot, prev = step % 2, (step + 1) % 2
        if step == 0:
            source = chunk_of(step)
        else:
            pltpu.make_async_remote_copy(
                src_ref=send_buf.at[prev],
                dst_ref=recv_buf.at[prev],
                send_sem=send_sems.at[prev],
                recv_sem=recv_sems.at[prev],
                device_id=left,
                device_id_type=mesh_kind,
            ).wait_recv()
            target = land if step == n - 1 else send_buf.at[slot]
            target[...] = recv_buf[prev] + chunk_of(step)[...]
            if step <= n - 3:
                pl.semaphore_signal(free_sem, inc=1, device_id=left, device_id_type=mesh_kind)
            source = send_buf.at[slot]
        if step < n - 1:
            if step >= 2:
                pl.semaphore_wait(free_sem, 1)
            copy = pltpu.make_async_remote_copy(
                src_ref=source,
                dst_ref=recv_buf.at[slot],
                send_sem=send_sems.at[slot],
                recv_sem=recv_sems.at[slot],
                device_id=right,
                device_id_type=mesh_kind,
            )
            copy.start()
            copy.wait_send()


def fsdp_sum_kernel(n_z, n_y, part_ref, out_ref, xbuf, zrecv, zsend, ztot, yrecv, ysend, sems0, dsems, free_sems):
    me = lax.axis_index("fsdp")
    site = lax.axis_index("site")
    core = lax.rem(me, 2)
    chip = me // 2
    zc, yc = chip // n_y, lax.rem(chip, n_y)
    sibling = me + 1 - 2 * core

    def device(z, y):
        return (site, 2 * (lax.rem(z + n_z, n_z) * n_y + lax.rem(y + n_y, n_y)) + core)

    mesh_kind = pl.DeviceIdType.MESH
    z_left, z_right = device(zc - 1, yc), device(zc + 1, yc)
    y_left, y_right = device(zc, yc - 1), device(zc, yc + 1)
    barrier = pltpu.get_barrier_semaphore()
    for peer in ((site, sibling), z_left, z_right, y_left, y_right):
        pl.semaphore_signal(barrier, inc=1, device_id=peer, device_id_type=mesh_kind)
    pl.semaphore_wait(barrier, 5)
    swap = pltpu.make_async_remote_copy(
        src_ref=part_ref.at[1 - core],
        dst_ref=xbuf,
        send_sem=sems0.at[0],
        recv_sem=sems0.at[1],
        device_id=(site, sibling),
        device_id_type=mesh_kind,
    )
    swap.start()
    swap.wait()

    def add_own(index, carry):
        xbuf[index] = xbuf[index] + part_ref[core, index]
        return carry

    lax.fori_loop(0, n_z * n_y, add_own, 0)

    def z_chunk(step):
        column = lax.rem(zc - 1 - step + 2 * n_z, n_z)
        return xbuf.at[pl.ds(column * n_y, n_y)]

    ring_pass(n_z, z_left, z_right, z_chunk, ztot, zrecv, zsend, dsems.at[0], dsems.at[1], free_sems.at[0])

    def y_chunk(step):
        return ztot.at[lax.rem(yc - 1 - step + 2 * n_y, n_y)]

    ring_pass(n_y, y_left, y_right, y_chunk, out_ref, yrecv, ysend, dsems.at[2], dsems.at[3], free_sems.at[1])


def fsdp_sum(part, n_z):
    n_chip = part.shape[1]
    n_y = n_chip // n_z
    block = part.shape[2:]
    return pl.pallas_call(
        functools.partial(fsdp_sum_kernel, n_z, n_y),
        out_shape=jax.ShapeDtypeStruct(block, part.dtype),
        in_specs=[pl.BlockSpec(memory_space=pltpu.VMEM)],
        out_specs=pl.BlockSpec(memory_space=pltpu.VMEM),
        scratch_shapes=[
            pltpu.VMEM((n_chip,) + block, part.dtype),
            pltpu.VMEM((2, n_y) + block, part.dtype),
            pltpu.VMEM((2, n_y) + block, part.dtype),
            pltpu.VMEM((n_y,) + block, part.dtype),
            pltpu.VMEM((2,) + block, part.dtype),
            pltpu.VMEM((2,) + block, part.dtype),
            pltpu.SemaphoreType.DMA((2,)),
            pltpu.SemaphoreType.DMA((4, 2)),
            pltpu.SemaphoreType.REGULAR((2,)),
        ],
        compiler_params=pltpu.CompilerParams(collective_id=1, has_side_effects=True),
    )(part)


def site_sum(part):
    n_site = lax.axis_size("site")
    return pl.pallas_call(
        functools.partial(site_sum_kernel, n_site),
        out_shape=jax.ShapeDtypeStruct(part.shape, part.dtype),
        in_specs=[pl.BlockSpec(memory_space=pltpu.VMEM)],
        out_specs=pl.BlockSpec(memory_space=pltpu.VMEM),
        scratch_shapes=[
            pltpu.VMEM((n_site,) + part.shape, part.dtype),
            pltpu.SemaphoreType.DMA((n_site,)),
            pltpu.SemaphoreType.DMA((n_site,)),
        ],
        compiler_params=pltpu.CompilerParams(collective_id=0, has_side_effects=True),
    )(part)


def body(held_input, held_cotangent, proj_weight, stem_weight, seg_counts):
    group_size = lax.axis_size("fsdp")
    capacity = 2 * ((OWN_SEG + 2 * group_size - 1) // (2 * group_size))
    my_index = lax.axis_index("fsdp")
    inputs = held_input[0].astype(jnp.float32)
    cotangent = held_cotangent[0]
    row_mean = jnp.mean(inputs, axis=-1, keepdims=True)
    centered = inputs - row_mean
    variance = jnp.mean(centered * centered, axis=-1, keepdims=True)
    inverse = lax.rsqrt(variance + EPSILON)
    normed = centered * inverse
    normed_bf = normed.astype(jnp.bfloat16)
    rows_w = proj_weight.shape[0]
    taps_n, chans = stem_weight.shape[0], stem_weight.shape[1]
    joined = jnp.concatenate([proj_weight, stem_weight.reshape(taps_n * chans, D)], 0)
    gathered = lax.all_gather(joined, "fsdp", axis=0, tiled=False)
    rows_out = D // group_size
    partial = jnp.einsum(
        "rckj,rd->kcjd",
        normed_bf.reshape(normed_bf.shape[0], group_size // 2, 2, rows_out),
        cotangent,
        preferred_element_type=jnp.float32,
    )
    shard_sum = fsdp_sum(partial, N_Z)
    shard_sum, gathered = lax.optimization_barrier((shard_sum, gathered))
    full_weight = gathered[:, :rows_w].reshape(group_size * rows_w, D)
    stem_gathered = gathered[:, rows_w:].reshape(group_size, taps_n, chans, D)
    proj_back = lax.dot_general(
        cotangent,
        full_weight,
        (((1,), (1,)), ((), ())),
        preferred_element_type=jnp.float32,
    )
    input_grad = cotangent.astype(jnp.float32) + inverse * (
        proj_back
        - jnp.mean(proj_back, axis=-1, keepdims=True)
        - normed * jnp.mean(proj_back * normed, axis=-1, keepdims=True)
    )
    input_grad = input_grad.astype(jnp.bfloat16)
    counts = seg_counts[0]
    endings = jnp.cumsum(counts)
    starts = endings - counts
    slot_ids = jnp.arange(HOLD, dtype=jnp.int32)
    item_index = 2 * (slot_ids // 2 * group_size + my_index) + slot_ids % 2
    owner_ids = jnp.sum((item_index[:, None] >= endings[None, :]).astype(jnp.int32), axis=1)
    earlier = (slot_ids[None, :] < slot_ids[:, None]) & (owner_ids[None, :] == owner_ids[:, None])
    rank_ids = jnp.sum(earlier.astype(jnp.int32), axis=1)
    target = owner_ids * capacity + rank_ids
    positions = jnp.arange(group_size * capacity, dtype=jnp.int32)
    matched = target[None, :] == positions[:, None]
    filled = jnp.any(matched, axis=1)
    source = jnp.sum(jnp.where(matched, slot_ids[None, :], 0), axis=1)
    owner_hit = jnp.arange(group_size, dtype=jnp.int32) == my_index
    my_count = jnp.sum(jnp.where(owner_hit, counts, 0))
    my_start = jnp.sum(jnp.where(owner_hit, starts, 0))
    segment = jnp.arange(OWN_SEG, dtype=jnp.int32)
    is_live = segment < my_count
    holder = (my_start + segment) // 2 % group_size
    before = (
        (segment[None, :] < segment[:, None])
        & (holder[None, :] == holder[:, None])
        & is_live[None, :]
    )
    holder_rank = jnp.sum(before.astype(jnp.int32), axis=1)
    row_index = jnp.where(is_live, holder * capacity + holder_rank, 0)
    held_segments = input_grad.reshape(HOLD, SEG, D)
    zero_bf = jnp.zeros((), jnp.bfloat16)
    send_rows = jnp.where(filled[:, None, None], jnp.take(held_segments, source, axis=0), zero_bf)
    received = lax.all_to_all(
        send_rows.reshape(group_size, capacity, SEG, D),
        "fsdp",
        split_axis=0,
        concat_axis=0,
        tiled=True,
    )
    picked = jnp.take(received.reshape(group_size * capacity, SEG, D), row_index, axis=0)
    frames = jnp.where(is_live[:, None, None], picked, zero_bf).reshape(OWN_SEG * SEG, D)
    tap_terms = stem_taps(frames, stem_gathered)
    shifted = jnp.concatenate(
        [tap_terms[0][1:], jnp.zeros((1, tap_terms.shape[2]), jnp.float32)], 0
    )
    odd_rows = tap_terms[2] + shifted
    stem_rows = (
        jnp.stack([tap_terms[1], odd_rows], 1)
        .reshape(2 * OWN_SEG * SEG, tap_terms.shape[2])
        .astype(jnp.bfloat16)
    )
    shard_sum = site_sum(shard_sum)
    weight_grad = shard_sum / math.sqrt(lax.axis_size("site") * group_size * HOLD * SEG)
    return (stem_rows[None], weight_grad)


def solution(mesh):
    placed = (
        P("site", "fsdp", None),
        P("site", "fsdp", None),
        P("fsdp", None),
        P(None, "fsdp", None),
        P("site", None),
    )
    return jax.shard_map(
        body,
        mesh=mesh,
        in_specs=placed,
        out_specs=(P("site", "fsdp", None), P("fsdp", None)),
        check_vma=False,
    )
```

```python
import functools
import math

import jax
import jax.numpy as jnp
from jax import lax
from jax.experimental import pallas as pl
from jax.experimental.pallas import tpu as pltpu
from jax.sharding import PartitionSpec as P

D = 1536
SEG = 8
HOLD = 64
OWN_SEG = 128
N_Z = 8


EPSILON = 1e-05


def stem_taps(frames, stem_gathered):
    taps = jnp.einsum(
        "rd,fkcd->krfc", frames, stem_gathered, preferred_element_type=jnp.float32
    )
    return taps.reshape(taps.shape[0], taps.shape[1], -1)


def site_sum_kernel(n_site, part_ref, out_ref, slots, send_sems, recv_sems):
    me = lax.axis_index("site")
    col = lax.axis_index("fsdp")
    mesh_kind = pl.DeviceIdType.MESH
    barrier = pltpu.get_barrier_semaphore()
    for step in range(1, n_site):
        peer = lax.rem(me + step, n_site)
        pl.semaphore_signal(barrier, inc=1, device_id=(peer, col), device_id_type=mesh_kind)
    pl.semaphore_wait(barrier, n_site - 1)
    copies = []
    for step in range(1, n_site):
        peer = lax.rem(me + step, n_site)
        copy = pltpu.make_async_remote_copy(
            src_ref=part_ref,
            dst_ref=slots.at[me],
            send_sem=send_sems.at[step],
            recv_sem=recv_sems.at[me],
            device_id=(peer, col),
            device_id_type=mesh_kind,
        )
        copy.start()
        copies.append(copy)
    slots[me] = part_ref[...]
    for copy in copies:
        copy.wait_send()
    for step in range(1, n_site):
        src = lax.rem(me + step, n_site)
        pltpu.make_async_remote_copy(
            src_ref=part_ref,
            dst_ref=slots.at[src],
            send_sem=send_sems.at[0],
            recv_sem=recv_sems.at[src],
            device_id=(src, col),
            device_id_type=mesh_kind,
        ).wait_recv()
    total = slots[0]
    for index in range(1, n_site):
        total = total + slots[index]
    out_ref[...] = total


def ring_pass(n, lanes):
    mesh_kind = pl.DeviceIdType.MESH
    for step in range(n):
        slot, prev = step % 2, (step + 1) % 2
        sources = []
        for left, right, chunk_of, land, recv_buf, send_buf, recv_sems, send_sems, free_sem in lanes:
            if step == 0:
                sources.append(chunk_of(step))
                continue
            pltpu.make_async_remote_copy(
                src_ref=send_buf.at[prev],
                dst_ref=recv_buf.at[prev],
                send_sem=send_sems.at[prev],
                recv_sem=recv_sems.at[prev],
                device_id=left,
                device_id_type=mesh_kind,
            ).wait_recv()
            target = land if step == n - 1 else send_buf.at[slot]
            target[...] = recv_buf[prev] + chunk_of(step)[...]
            if step <= n - 3:
                pl.semaphore_signal(free_sem, inc=1, device_id=left, device_id_type=mesh_kind)
            sources.append(send_buf.at[slot])
        if step == n - 1:
            break
        copies = []
        for lane, source in zip(lanes, sources):
            left, right, chunk_of, land, recv_buf, send_buf, recv_sems, send_sems, free_sem = lane
            if step >= 2:
                pl.semaphore_wait(free_sem, 1)
            copy = pltpu.make_async_remote_copy(
                src_ref=source,
                dst_ref=recv_buf.at[slot],
                send_sem=send_sems.at[slot],
                recv_sem=recv_sems.at[slot],
                device_id=right,
                device_id_type=mesh_kind,
            )
            copy.start()
            copies.append(copy)
        for copy in copies:
            copy.wait_send()


def fsdp_sum_kernel(n_z, n_y, part_ref, out_ref, xbuf, zrecv, zsend, ztot, yrecv, ysend, sems0, dsems, free_sems):
    me = lax.axis_index("fsdp")
    site = lax.axis_index("site")
    core = lax.rem(me, 2)
    chip = me // 2
    zc, yc = chip // n_y, lax.rem(chip, n_y)
    sibling = me + 1 - 2 * core

    def device(z, y):
        return (site, 2 * (lax.rem(z + n_z, n_z) * n_y + lax.rem(y + n_y, n_y)) + core)

    mesh_kind = pl.DeviceIdType.MESH
    barrier = pltpu.get_barrier_semaphore()
    peers = ((site, sibling), device(zc - 1, yc), device(zc + 1, yc), device(zc, yc - 1), device(zc, yc + 1))
    for peer in peers:
        pl.semaphore_signal(barrier, inc=1, device_id=peer, device_id_type=mesh_kind)
    pl.semaphore_wait(barrier, len(peers))
    swap = pltpu.make_async_remote_copy(
        src_ref=part_ref.at[1 - core],
        dst_ref=xbuf,
        send_sem=sems0.at[0],
        recv_sem=sems0.at[1],
        device_id=(site, sibling),
        device_id_type=mesh_kind,
    )
    swap.start()
    swap.wait()

    def add_own(index, carry):
        xbuf[index] = xbuf[index] + part_ref[core, index]
        return carry

    lax.fori_loop(0, n_z * n_y, add_own, 0)

    z_lanes, y_lanes = [], []
    for lane, way in enumerate((1, -1)):

        def z_chunk(step, lane=lane, way=way):
            column = lax.rem(zc - way * (1 + step) + 2 * n_z, n_z)
            return xbuf.at[pl.ds(column * n_y, n_y), lane]

        def y_chunk(step, lane=lane, way=way):
            return ztot.at[lax.rem(yc - way * (1 + step) + 2 * n_y, n_y), lane]

        z_lanes.append((
            device(zc - way, yc), device(zc + way, yc), z_chunk, ztot.at[:, lane],
            zrecv.at[lane], zsend.at[lane], dsems.at[0, lane, 0], dsems.at[0, lane, 1], free_sems.at[0, lane],
        ))
        y_lanes.append((
            device(zc, yc - way), device(zc, yc + way), y_chunk, out_ref.at[lane],
            yrecv.at[lane], ysend.at[lane], dsems.at[1, lane, 0], dsems.at[1, lane, 1], free_sems.at[1, lane],
        ))
    ring_pass(n_z, z_lanes)
    ring_pass(n_y, y_lanes)


def fsdp_sum(part, n_z):
    n_chip = part.shape[1]
    n_y = n_chip // n_z
    block = part.shape[2:]
    lane_block = part.shape[3:]
    return pl.pallas_call(
        functools.partial(fsdp_sum_kernel, n_z, n_y),
        out_shape=jax.ShapeDtypeStruct(block, part.dtype),
        in_specs=[pl.BlockSpec(memory_space=pltpu.VMEM)],
        out_specs=pl.BlockSpec(memory_space=pltpu.VMEM),
        scratch_shapes=[
            pltpu.VMEM((n_chip,) + block, part.dtype),
            pltpu.VMEM((2, 2, n_y) + lane_block, part.dtype),
            pltpu.VMEM((2, 2, n_y) + lane_block, part.dtype),
            pltpu.VMEM((n_y,) + block, part.dtype),
            pltpu.VMEM((2, 2) + lane_block, part.dtype),
            pltpu.VMEM((2, 2) + lane_block, part.dtype),
            pltpu.SemaphoreType.DMA((2,)),
            pltpu.SemaphoreType.DMA((2, 2, 2, 2)),
            pltpu.SemaphoreType.REGULAR((2, 2)),
        ],
        compiler_params=pltpu.CompilerParams(collective_id=1, has_side_effects=True),
    )(part)


def site_sum(part):
    n_site = lax.axis_size("site")
    return pl.pallas_call(
        functools.partial(site_sum_kernel, n_site),
        out_shape=jax.ShapeDtypeStruct(part.shape, part.dtype),
        in_specs=[pl.BlockSpec(memory_space=pltpu.VMEM)],
        out_specs=pl.BlockSpec(memory_space=pltpu.VMEM),
        scratch_shapes=[
            pltpu.VMEM((n_site,) + part.shape, part.dtype),
            pltpu.SemaphoreType.DMA((n_site,)),
            pltpu.SemaphoreType.DMA((n_site,)),
        ],
        compiler_params=pltpu.CompilerParams(collective_id=0, has_side_effects=True),
    )(part)


def body(held_input, held_cotangent, proj_weight, stem_weight, seg_counts):
    group_size = lax.axis_size("fsdp")
    capacity = 2 * ((OWN_SEG + 2 * group_size - 1) // (2 * group_size))
    my_index = lax.axis_index("fsdp")
    inputs = held_input[0].astype(jnp.float32)
    cotangent = held_cotangent[0]
    row_mean = jnp.mean(inputs, axis=-1, keepdims=True)
    centered = inputs - row_mean
    variance = jnp.mean(centered * centered, axis=-1, keepdims=True)
    inverse = lax.rsqrt(variance + EPSILON)
    normed = centered * inverse
    normed_bf = normed.astype(jnp.bfloat16)
    rows_w = proj_weight.shape[0]
    taps_n, chans = stem_weight.shape[0], stem_weight.shape[1]
    joined = jnp.concatenate([proj_weight, stem_weight.reshape(taps_n * chans, D)], 0)
    gathered = lax.all_gather(joined, "fsdp", axis=0, tiled=False)
    rows_out = D // group_size
    partial = jnp.einsum(
        "rckj,rhd->kchjd",
        normed_bf.reshape(normed_bf.shape[0], group_size // 2, 2, rows_out),
        cotangent.reshape(cotangent.shape[0], 2, D // 2),
        preferred_element_type=jnp.float32,
    )
    shard_sum = fsdp_sum(partial, N_Z).transpose(1, 0, 2).reshape(rows_out, D)
    shard_sum, gathered = lax.optimization_barrier((shard_sum, gathered))
    full_weight = gathered[:, :rows_w].reshape(group_size * rows_w, D)
    stem_gathered = gathered[:, rows_w:].reshape(group_size, taps_n, chans, D)
    proj_back = lax.dot_general(
        cotangent,
        full_weight,
        (((1,), (1,)), ((), ())),
        preferred_element_type=jnp.float32,
    )
    input_grad = cotangent.astype(jnp.float32) + inverse * (
        proj_back
        - jnp.mean(proj_back, axis=-1, keepdims=True)
        - normed * jnp.mean(proj_back * normed, axis=-1, keepdims=True)
    )
    input_grad = input_grad.astype(jnp.bfloat16)
    counts = seg_counts[0]
    endings = jnp.cumsum(counts)
    starts = endings - counts
    slot_ids = jnp.arange(HOLD, dtype=jnp.int32)
    item_index = 2 * (slot_ids // 2 * group_size + my_index) + slot_ids % 2
    owner_ids = jnp.sum((item_index[:, None] >= endings[None, :]).astype(jnp.int32), axis=1)
    earlier = (slot_ids[None, :] < slot_ids[:, None]) & (owner_ids[None, :] == owner_ids[:, None])
    rank_ids = jnp.sum(earlier.astype(jnp.int32), axis=1)
    target = owner_ids * capacity + rank_ids
    positions = jnp.arange(group_size * capacity, dtype=jnp.int32)
    matched = target[None, :] == positions[:, None]
    filled = jnp.any(matched, axis=1)
    source = jnp.sum(jnp.where(matched, slot_ids[None, :], 0), axis=1)
    owner_hit = jnp.arange(group_size, dtype=jnp.int32) == my_index
    my_count = jnp.sum(jnp.where(owner_hit, counts, 0))
    my_start = jnp.sum(jnp.where(owner_hit, starts, 0))
    segment = jnp.arange(OWN_SEG, dtype=jnp.int32)
    is_live = segment < my_count
    holder = (my_start + segment) // 2 % group_size
    before = (
        (segment[None, :] < segment[:, None])
        & (holder[None, :] == holder[:, None])
        & is_live[None, :]
    )
    holder_rank = jnp.sum(before.astype(jnp.int32), axis=1)
    row_index = jnp.where(is_live, holder * capacity + holder_rank, 0)
    held_segments = input_grad.reshape(HOLD, SEG, D)
    zero_bf = jnp.zeros((), jnp.bfloat16)
    send_rows = jnp.where(filled[:, None, None], jnp.take(held_segments, source, axis=0), zero_bf)
    received = lax.all_to_all(
        send_rows.reshape(group_size, capacity, SEG, D),
        "fsdp",
        split_axis=0,
        concat_axis=0,
        tiled=True,
    )
    picked = jnp.take(received.reshape(group_size * capacity, SEG, D), row_index, axis=0)
    frames = jnp.where(is_live[:, None, None], picked, zero_bf).reshape(OWN_SEG * SEG, D)
    tap_terms = stem_taps(frames, stem_gathered)
    shifted = jnp.concatenate(
        [tap_terms[0][1:], jnp.zeros((1, tap_terms.shape[2]), jnp.float32)], 0
    )
    odd_rows = tap_terms[2] + shifted
    stem_rows = (
        jnp.stack([tap_terms[1], odd_rows], 1)
        .reshape(2 * OWN_SEG * SEG, tap_terms.shape[2])
        .astype(jnp.bfloat16)
    )
    shard_sum = site_sum(shard_sum)
    weight_grad = shard_sum / math.sqrt(lax.axis_size("site") * group_size * HOLD * SEG)
    return (stem_rows[None], weight_grad)


def solution(mesh):
    placed = (
        P("site", "fsdp", None),
        P("site", "fsdp", None),
        P("fsdp", None),
        P(None, "fsdp", None),
        P("site", None),
    )
    return jax.shard_map(
        body,
        mesh=mesh,
        in_specs=placed,
        out_specs=(P("site", "fsdp", None), P("fsdp", None)),
        check_vma=False,
    )
```

```python
import functools
import math

import jax
import jax.numpy as jnp
from jax import lax
from jax.experimental import pallas as pl
from jax.experimental.pallas import tpu as pltpu
from jax.sharding import PartitionSpec as P

D = 1536
SEG = 8
HOLD = 64
OWN_SEG = 128
N_Z = 8


EPSILON = 1e-05


def stem_taps(frames, stem_gathered):
    taps = jnp.einsum(
        "rd,fkcd->krfc", frames, stem_gathered, preferred_element_type=jnp.float32
    )
    return taps.reshape(taps.shape[0], taps.shape[1], -1)


def ring_pass(n, lanes):
    mesh_kind = pl.DeviceIdType.MESH
    for step in range(n):
        slot, prev = step % 2, (step + 1) % 2
        sources = []
        for left, right, chunk_of, land, recv_buf, send_buf, recv_sems, send_sems, free_sem in lanes:
            if step == 0:
                sources.append(chunk_of(step))
                continue
            pltpu.make_async_remote_copy(
                src_ref=send_buf.at[prev],
                dst_ref=recv_buf.at[prev],
                send_sem=send_sems.at[prev],
                recv_sem=recv_sems.at[prev],
                device_id=left,
                device_id_type=mesh_kind,
            ).wait_recv()
            target = land if step == n - 1 else send_buf.at[slot]
            target[...] = recv_buf[prev] + chunk_of(step)[...]
            if step <= n - 3:
                pl.semaphore_signal(free_sem, inc=1, device_id=left, device_id_type=mesh_kind)
            sources.append(send_buf.at[slot])
        if step == n - 1:
            break
        copies = []
        for lane, source in zip(lanes, sources):
            left, right, chunk_of, land, recv_buf, send_buf, recv_sems, send_sems, free_sem = lane
            if step >= 2:
                pl.semaphore_wait(free_sem, 1)
            copy = pltpu.make_async_remote_copy(
                src_ref=source,
                dst_ref=recv_buf.at[slot],
                send_sem=send_sems.at[slot],
                recv_sem=recv_sems.at[slot],
                device_id=right,
                device_id_type=mesh_kind,
            )
            copy.start()
            copies.append(copy)
        for copy in copies:
            copy.wait_send()


def z_sum_kernel(n_z, n_y, part_ref, ztot, xbuf, zrecv, zsend, sems0, dsems, free_sems):
    me = lax.axis_index("fsdp")
    site = lax.axis_index("site")
    core = lax.rem(me, 2)
    chip = me // 2
    zc, yc = chip // n_y, lax.rem(chip, n_y)
    sibling = me + 1 - 2 * core

    def device(z):
        return (site, 2 * (lax.rem(z + n_z, n_z) * n_y + yc) + core)

    mesh_kind = pl.DeviceIdType.MESH
    barrier = pltpu.get_barrier_semaphore()
    peers = ((site, sibling), device(zc - 1), device(zc + 1))
    for peer in peers:
        pl.semaphore_signal(barrier, inc=1, device_id=peer, device_id_type=mesh_kind)
    pl.semaphore_wait(barrier, len(peers))
    swap = pltpu.make_async_remote_copy(
        src_ref=part_ref.at[1 - core],
        dst_ref=xbuf,
        send_sem=sems0.at[0],
        recv_sem=sems0.at[1],
        device_id=(site, sibling),
        device_id_type=mesh_kind,
    )
    swap.start()
    swap.wait()

    def add_own(index, carry):
        xbuf[index] = xbuf[index] + part_ref[core, index]
        return carry

    lax.fori_loop(0, n_z * n_y, add_own, 0)
    lanes = []
    for lane, way in enumerate((1, -1)):

        def z_chunk(step, lane=lane, way=way):
            column = lax.rem(zc - way * (1 + step) + 2 * n_z, n_z)
            return xbuf.at[pl.ds(column * n_y, n_y), lane]

        lanes.append((
            device(zc - way), device(zc + way), z_chunk, ztot.at[:, lane],
            zrecv.at[lane], zsend.at[lane], dsems.at[lane, 0], dsems.at[lane, 1], free_sems.at[lane],
        ))
    ring_pass(n_z, lanes)


def y_site_kernel(n_y, n_site, ztot, out_ref, yrecv, ysend, ytot, slots, dsems, free_sems, site_send, site_recv):
    me = lax.axis_index("fsdp")
    site = lax.axis_index("site")
    core = lax.rem(me, 2)
    chip = me // 2
    zc, yc = chip // n_y, lax.rem(chip, n_y)

    def device(y):
        return (site, 2 * (zc * n_y + lax.rem(y + n_y, n_y)) + core)

    mesh_kind = pl.DeviceIdType.MESH
    barrier = pltpu.get_barrier_semaphore()
    peers = [device(yc - 1), device(yc + 1)]
    for step in range(1, n_site):
        peers.append((lax.rem(site + step, n_site), me))
    for peer in peers:
        pl.semaphore_signal(barrier, inc=1, device_id=peer, device_id_type=mesh_kind)
    pl.semaphore_wait(barrier, len(peers))
    lanes = []
    for lane, way in enumerate((1, -1)):

        def y_chunk(step, lane=lane, way=way):
            return ztot.at[lax.rem(yc - way * (1 + step) + 2 * n_y, n_y), lane]

        lanes.append((
            device(yc - way), device(yc + way), y_chunk, ytot.at[lane],
            yrecv.at[lane], ysend.at[lane], dsems.at[lane, 0], dsems.at[lane, 1], free_sems.at[lane],
        ))
    ring_pass(n_y, lanes)
    copies = []
    for step in range(1, n_site):
        peer = lax.rem(site + step, n_site)
        copy = pltpu.make_async_remote_copy(
            src_ref=ytot,
            dst_ref=slots.at[site],
            send_sem=site_send.at[step],
            recv_sem=site_recv.at[site],
            device_id=(peer, me),
            device_id_type=mesh_kind,
        )
        copy.start()
        copies.append(copy)
    slots[site] = ytot[...]
    for copy in copies:
        copy.wait_send()
    for step in range(1, n_site):
        src = lax.rem(site + step, n_site)
        pltpu.make_async_remote_copy(
            src_ref=ytot,
            dst_ref=slots.at[src],
            send_sem=site_send.at[0],
            recv_sem=site_recv.at[src],
            device_id=(src, me),
            device_id_type=mesh_kind,
        ).wait_recv()
    total = slots[0]
    for index in range(1, n_site):
        total = total + slots[index]
    out_ref[...] = total


def z_sum(part, n_z):
    n_chip = part.shape[1]
    n_y = n_chip // n_z
    block = part.shape[2:]
    lane_block = part.shape[3:]
    return pl.pallas_call(
        functools.partial(z_sum_kernel, n_z, n_y),
        out_shape=jax.ShapeDtypeStruct((n_y,) + block, part.dtype),
        in_specs=[pl.BlockSpec(memory_space=pltpu.VMEM)],
        out_specs=pl.BlockSpec(memory_space=pltpu.VMEM),
        scratch_shapes=[
            pltpu.VMEM((n_chip,) + block, part.dtype),
            pltpu.VMEM((2, 2, n_y) + lane_block, part.dtype),
            pltpu.VMEM((2, 2, n_y) + lane_block, part.dtype),
            pltpu.SemaphoreType.DMA((2,)),
            pltpu.SemaphoreType.DMA((2, 2, 2)),
            pltpu.SemaphoreType.REGULAR((2,)),
        ],
        compiler_params=pltpu.CompilerParams(collective_id=1, has_side_effects=True),
    )(part)


def y_site_sum(ztot):
    n_y = ztot.shape[0]
    n_site = lax.axis_size("site")
    block = ztot.shape[1:]
    lane_block = ztot.shape[2:]
    return pl.pallas_call(
        functools.partial(y_site_kernel, n_y, n_site),
        out_shape=jax.ShapeDtypeStruct(block, ztot.dtype),
        in_specs=[pl.BlockSpec(memory_space=pltpu.VMEM)],
        out_specs=pl.BlockSpec(memory_space=pltpu.VMEM),
        scratch_shapes=[
            pltpu.VMEM((2, 2) + lane_block, ztot.dtype),
            pltpu.VMEM((2, 2) + lane_block, ztot.dtype),
            pltpu.VMEM(block, ztot.dtype),
            pltpu.VMEM((n_site,) + block, ztot.dtype),
            pltpu.SemaphoreType.DMA((2, 2, 2)),
            pltpu.SemaphoreType.REGULAR((2,)),
            pltpu.SemaphoreType.DMA((n_site,)),
            pltpu.SemaphoreType.DMA((n_site,)),
        ],
        compiler_params=pltpu.CompilerParams(collective_id=2, has_side_effects=True),
    )(ztot)


def body(held_input, held_cotangent, proj_weight, stem_weight, seg_counts):
    group_size = lax.axis_size("fsdp")
    capacity = 2 * ((OWN_SEG + 2 * group_size - 1) // (2 * group_size))
    my_index = lax.axis_index("fsdp")
    inputs = held_input[0].astype(jnp.float32)
    cotangent = held_cotangent[0]
    row_mean = jnp.mean(inputs, axis=-1, keepdims=True)
    centered = inputs - row_mean
    variance = jnp.mean(centered * centered, axis=-1, keepdims=True)
    inverse = lax.rsqrt(variance + EPSILON)
    normed = centered * inverse
    normed_bf = normed.astype(jnp.bfloat16)
    rows_w = proj_weight.shape[0]
    taps_n, chans = stem_weight.shape[0], stem_weight.shape[1]
    joined = jnp.concatenate([proj_weight, stem_weight.reshape(taps_n * chans, D)], 0)
    gathered = lax.all_gather(joined, "fsdp", axis=0, tiled=False)
    rows_out = D // group_size
    partial = jnp.einsum(
        "rckj,rhd->kchjd",
        normed_bf.reshape(normed_bf.shape[0], group_size // 2, 2, rows_out),
        cotangent.reshape(cotangent.shape[0], 2, D // 2),
        preferred_element_type=jnp.float32,
    )
    z_total = z_sum(partial, N_Z)
    z_total, gathered = lax.optimization_barrier((z_total, gathered))
    full_weight = gathered[:, :rows_w].reshape(group_size * rows_w, D)
    stem_gathered = gathered[:, rows_w:].reshape(group_size, taps_n, chans, D)
    proj_back = lax.dot_general(
        cotangent,
        full_weight,
        (((1,), (1,)), ((), ())),
        preferred_element_type=jnp.float32,
    )
    input_grad = cotangent.astype(jnp.float32) + inverse * (
        proj_back
        - jnp.mean(proj_back, axis=-1, keepdims=True)
        - normed * jnp.mean(proj_back * normed, axis=-1, keepdims=True)
    )
    input_grad = input_grad.astype(jnp.bfloat16)
    counts = seg_counts[0]
    endings = jnp.cumsum(counts)
    starts = endings - counts
    slot_ids = jnp.arange(HOLD, dtype=jnp.int32)
    item_index = 2 * (slot_ids // 2 * group_size + my_index) + slot_ids % 2
    owner_ids = jnp.sum((item_index[:, None] >= endings[None, :]).astype(jnp.int32), axis=1)
    earlier = (slot_ids[None, :] < slot_ids[:, None]) & (owner_ids[None, :] == owner_ids[:, None])
    rank_ids = jnp.sum(earlier.astype(jnp.int32), axis=1)
    target = owner_ids * capacity + rank_ids
    positions = jnp.arange(group_size * capacity, dtype=jnp.int32)
    matched = target[None, :] == positions[:, None]
    filled = jnp.any(matched, axis=1)
    source = jnp.sum(jnp.where(matched, slot_ids[None, :], 0), axis=1)
    owner_hit = jnp.arange(group_size, dtype=jnp.int32) == my_index
    my_count = jnp.sum(jnp.where(owner_hit, counts, 0))
    my_start = jnp.sum(jnp.where(owner_hit, starts, 0))
    segment = jnp.arange(OWN_SEG, dtype=jnp.int32)
    is_live = segment < my_count
    holder = (my_start + segment) // 2 % group_size
    before = (
        (segment[None, :] < segment[:, None])
        & (holder[None, :] == holder[:, None])
        & is_live[None, :]
    )
    holder_rank = jnp.sum(before.astype(jnp.int32), axis=1)
    row_index = jnp.where(is_live, holder * capacity + holder_rank, 0)
    held_segments = input_grad.reshape(HOLD, SEG, D)
    zero_bf = jnp.zeros((), jnp.bfloat16)
    send_rows = jnp.where(filled[:, None, None], jnp.take(held_segments, source, axis=0), zero_bf)
    received = lax.all_to_all(
        send_rows.reshape(group_size, capacity, SEG, D),
        "fsdp",
        split_axis=0,
        concat_axis=0,
        tiled=True,
    )
    picked = jnp.take(received.reshape(group_size * capacity, SEG, D), row_index, axis=0)
    frames = jnp.where(is_live[:, None, None], picked, zero_bf).reshape(OWN_SEG * SEG, D)
    tap_terms = stem_taps(frames, stem_gathered)
    shifted = jnp.concatenate(
        [tap_terms[0][1:], jnp.zeros((1, tap_terms.shape[2]), jnp.float32)], 0
    )
    odd_rows = tap_terms[2] + shifted
    stem_rows = (
        jnp.stack([tap_terms[1], odd_rows], 1)
        .reshape(2 * OWN_SEG * SEG, tap_terms.shape[2])
        .astype(jnp.bfloat16)
    )
    shard_sum = y_site_sum(z_total).transpose(1, 0, 2).reshape(rows_out, D)
    weight_grad = shard_sum / math.sqrt(lax.axis_size("site") * group_size * HOLD * SEG)
    return (stem_rows[None], weight_grad)


def solution(mesh):
    placed = (
        P("site", "fsdp", None),
        P("site", "fsdp", None),
        P("fsdp", None),
        P(None, "fsdp", None),
        P("site", None),
    )
    return jax.shard_map(
        body,
        mesh=mesh,
        in_specs=placed,
        out_specs=(P("site", "fsdp", None), P("fsdp", None)),
        check_vma=False,
    )
```

```python
import functools
import math

import jax
import jax.numpy as jnp
from jax import lax
from jax.experimental import pallas as pl
from jax.experimental.pallas import tpu as pltpu
from jax.sharding import PartitionSpec as P

D = 1536
SEG = 8
HOLD = 64
OWN_SEG = 128
N_Z = 8


EPSILON = 1e-05


def stem_taps(frames, stem_gathered):
    taps = jnp.einsum(
        "rd,fkcd->krfc", frames, stem_gathered, preferred_element_type=jnp.float32
    )
    return taps.reshape(taps.shape[0], taps.shape[1], -1)


def ring_pass(n, lanes, prepare=None):
    mesh_kind = pl.DeviceIdType.MESH
    for step in range(n):
        slot, prev = step % 2, (step + 1) % 2
        sources = []
        for lane_index, lane in enumerate(lanes):
            left, right, chunk_of, land, recv_buf, send_buf, recv_sems, send_sems, free_sem = lane
            if prepare is not None:
                prepare(lane_index, step)
            if step == 0:
                sources.append(chunk_of(step))
                continue
            pltpu.make_async_remote_copy(
                src_ref=send_buf.at[prev],
                dst_ref=recv_buf.at[prev],
                send_sem=send_sems.at[prev],
                recv_sem=recv_sems.at[prev],
                device_id=left,
                device_id_type=mesh_kind,
            ).wait_recv()
            target = land if step == n - 1 else send_buf.at[slot]
            target[...] = recv_buf[prev] + chunk_of(step)[...]
            if step <= n - 3:
                pl.semaphore_signal(free_sem, inc=1, device_id=left, device_id_type=mesh_kind)
            sources.append(send_buf.at[slot])
        if step == n - 1:
            break
        copies = []
        for lane, source in zip(lanes, sources):
            left, right, chunk_of, land, recv_buf, send_buf, recv_sems, send_sems, free_sem = lane
            if step >= 2:
                pl.semaphore_wait(free_sem, 1)
            copy = pltpu.make_async_remote_copy(
                src_ref=source,
                dst_ref=recv_buf.at[slot],
                send_sem=send_sems.at[slot],
                recv_sem=recv_sems.at[slot],
                device_id=right,
                device_id_type=mesh_kind,
            )
            copy.start()
            copies.append(copy)
        for copy in copies:
            copy.wait_send()


def z_sum_kernel(n_z, n_y, lo_ref, hi_ref, ztot, xbuf, zrecv, zsend, swap_sems, dsems, free_sems):
    me = lax.axis_index("fsdp")
    site = lax.axis_index("site")
    core = lax.rem(me, 2)
    chip = me // 2
    zc, yc = chip // n_y, lax.rem(chip, n_y)
    sibling = me + 1 - 2 * core

    def device(z):
        return (site, 2 * (lax.rem(z + n_z, n_z) * n_y + yc) + core)

    mesh_kind = pl.DeviceIdType.MESH
    barrier = pltpu.get_barrier_semaphore()
    peers = ((site, sibling), device(zc - 1), device(zc + 1))
    for peer in peers:
        pl.semaphore_signal(barrier, inc=1, device_id=peer, device_id_type=mesh_kind)
    pl.semaphore_wait(barrier, len(peers))
    ways = (1, -1)
    parts = (lo_ref, hi_ref)

    def rows(lane, step):
        column = lax.rem(zc - ways[lane] * (1 + step) + 2 * n_z, n_z)
        return pl.ds(column * n_y, n_y)

    def swap(lane, step):
        return pltpu.make_async_remote_copy(
            src_ref=parts[lane].at[1 - core, rows(lane, step)],
            dst_ref=xbuf.at[rows(lane, step), lane],
            send_sem=swap_sems.at[lane, step, 0],
            recv_sem=swap_sems.at[lane, step, 1],
            device_id=(site, sibling),
            device_id_type=mesh_kind,
        )

    for step in range(n_z):
        for lane in range(2):
            swap(lane, step).start()

    def prepare(lane, step):
        swap(lane, step).wait_recv()
        here = rows(lane, step)
        xbuf[here, lane] = xbuf[here, lane] + parts[lane][core, here]

    lanes = []
    for lane, way in enumerate(ways):

        def z_chunk(step, lane=lane):
            return xbuf.at[rows(lane, step), lane]

        lanes.append((
            device(zc - way), device(zc + way), z_chunk, ztot.at[:, lane],
            zrecv.at[lane], zsend.at[lane], dsems.at[lane, 0], dsems.at[lane, 1], free_sems.at[lane],
        ))
    ring_pass(n_z, lanes, prepare)
    for step in range(n_z):
        for lane in range(2):
            swap(lane, step).wait_send()


def y_site_kernel(n_y, n_site, ztot, out_ref, yrecv, ysend, ytot, slots, dsems, free_sems, site_send, site_recv):
    me = lax.axis_index("fsdp")
    site = lax.axis_index("site")
    core = lax.rem(me, 2)
    chip = me // 2
    zc, yc = chip // n_y, lax.rem(chip, n_y)

    def device(y):
        return (site, 2 * (zc * n_y + lax.rem(y + n_y, n_y)) + core)

    mesh_kind = pl.DeviceIdType.MESH
    barrier = pltpu.get_barrier_semaphore()
    peers = [device(yc - 1), device(yc + 1)]
    for step in range(1, n_site):
        peers.append((lax.rem(site + step, n_site), me))
    for peer in peers:
        pl.semaphore_signal(barrier, inc=1, device_id=peer, device_id_type=mesh_kind)
    pl.semaphore_wait(barrier, len(peers))
    lanes = []
    for lane, way in enumerate((1, -1)):

        def y_chunk(step, lane=lane, way=way):
            return ztot.at[lax.rem(yc - way * (1 + step) + 2 * n_y, n_y), lane]

        lanes.append((
            device(yc - way), device(yc + way), y_chunk, ytot.at[lane],
            yrecv.at[lane], ysend.at[lane], dsems.at[lane, 0], dsems.at[lane, 1], free_sems.at[lane],
        ))
    ring_pass(n_y, lanes)
    copies = []
    for step in range(1, n_site):
        peer = lax.rem(site + step, n_site)
        copy = pltpu.make_async_remote_copy(
            src_ref=ytot,
            dst_ref=slots.at[site],
            send_sem=site_send.at[step],
            recv_sem=site_recv.at[site],
            device_id=(peer, me),
            device_id_type=mesh_kind,
        )
        copy.start()
        copies.append(copy)
    slots[site] = ytot[...]
    for copy in copies:
        copy.wait_send()
    for step in range(1, n_site):
        src = lax.rem(site + step, n_site)
        pltpu.make_async_remote_copy(
            src_ref=ytot,
            dst_ref=slots.at[src],
            send_sem=site_send.at[0],
            recv_sem=site_recv.at[src],
            device_id=(src, me),
            device_id_type=mesh_kind,
        ).wait_recv()
    total = slots[0]
    for index in range(1, n_site):
        total = total + slots[index]
    out_ref[...] = total


def z_sum(lo, hi, n_z):
    n_chip = lo.shape[1]
    n_y = n_chip // n_z
    lane_block = lo.shape[2:]
    block = (2,) + lane_block
    return pl.pallas_call(
        functools.partial(z_sum_kernel, n_z, n_y),
        out_shape=jax.ShapeDtypeStruct((n_y,) + block, lo.dtype),
        in_specs=[pl.BlockSpec(memory_space=pltpu.VMEM)] * 2,
        out_specs=pl.BlockSpec(memory_space=pltpu.VMEM),
        scratch_shapes=[
            pltpu.VMEM((n_chip,) + block, lo.dtype),
            pltpu.VMEM((2, 2, n_y) + lane_block, lo.dtype),
            pltpu.VMEM((2, 2, n_y) + lane_block, lo.dtype),
            pltpu.SemaphoreType.DMA((2, n_z, 2)),
            pltpu.SemaphoreType.DMA((2, 2, 2)),
            pltpu.SemaphoreType.REGULAR((2,)),
        ],
        compiler_params=pltpu.CompilerParams(collective_id=1, has_side_effects=True),
    )(lo, hi)


def y_site_sum(ztot):
    n_y = ztot.shape[0]
    n_site = lax.axis_size("site")
    block = ztot.shape[1:]
    lane_block = ztot.shape[2:]
    return pl.pallas_call(
        functools.partial(y_site_kernel, n_y, n_site),
        out_shape=jax.ShapeDtypeStruct(block, ztot.dtype),
        in_specs=[pl.BlockSpec(memory_space=pltpu.VMEM)],
        out_specs=pl.BlockSpec(memory_space=pltpu.VMEM),
        scratch_shapes=[
            pltpu.VMEM((2, 2) + lane_block, ztot.dtype),
            pltpu.VMEM((2, 2) + lane_block, ztot.dtype),
            pltpu.VMEM(block, ztot.dtype),
            pltpu.VMEM((n_site,) + block, ztot.dtype),
            pltpu.SemaphoreType.DMA((2, 2, 2)),
            pltpu.SemaphoreType.REGULAR((2,)),
            pltpu.SemaphoreType.DMA((n_site,)),
            pltpu.SemaphoreType.DMA((n_site,)),
        ],
        compiler_params=pltpu.CompilerParams(collective_id=2, has_side_effects=True),
    )(ztot)


def body(held_input, held_cotangent, proj_weight, stem_weight, seg_counts):
    group_size = lax.axis_size("fsdp")
    capacity = 2 * ((OWN_SEG + 2 * group_size - 1) // (2 * group_size))
    my_index = lax.axis_index("fsdp")
    inputs = held_input[0].astype(jnp.float32)
    cotangent = held_cotangent[0]
    row_mean = jnp.mean(inputs, axis=-1, keepdims=True)
    centered = inputs - row_mean
    variance = jnp.mean(centered * centered, axis=-1, keepdims=True)
    inverse = lax.rsqrt(variance + EPSILON)
    normed = centered * inverse
    normed_bf = normed.astype(jnp.bfloat16)
    rows_w = proj_weight.shape[0]
    taps_n, chans = stem_weight.shape[0], stem_weight.shape[1]
    joined = jnp.concatenate([proj_weight, stem_weight.reshape(taps_n * chans, D)], 0)
    gathered = lax.all_gather(joined, "fsdp", axis=0, tiled=False)
    rows_out = D // group_size
    by_core = normed_bf.reshape(normed_bf.shape[0], group_size // 2, 2, rows_out)
    halves = [
        jnp.einsum("rckj,rd->kcjd", by_core, cotangent[:, part * (D // 2):(part + 1) * (D // 2)],
                   preferred_element_type=jnp.float32)
        for part in range(2)
    ]
    z_total = z_sum(halves[0], halves[1], N_Z)
    z_total, gathered = lax.optimization_barrier((z_total, gathered))
    full_weight = gathered[:, :rows_w].reshape(group_size * rows_w, D)
    stem_gathered = gathered[:, rows_w:].reshape(group_size, taps_n, chans, D)
    proj_back = lax.dot_general(
        cotangent,
        full_weight,
        (((1,), (1,)), ((), ())),
        preferred_element_type=jnp.float32,
    )
    input_grad = cotangent.astype(jnp.float32) + inverse * (
        proj_back
        - jnp.mean(proj_back, axis=-1, keepdims=True)
        - normed * jnp.mean(proj_back * normed, axis=-1, keepdims=True)
    )
    input_grad = input_grad.astype(jnp.bfloat16)
    counts = seg_counts[0]
    endings = jnp.cumsum(counts)
    starts = endings - counts
    slot_ids = jnp.arange(HOLD, dtype=jnp.int32)
    item_index = 2 * (slot_ids // 2 * group_size + my_index) + slot_ids % 2
    owner_ids = jnp.sum((item_index[:, None] >= endings[None, :]).astype(jnp.int32), axis=1)
    earlier = (slot_ids[None, :] < slot_ids[:, None]) & (owner_ids[None, :] == owner_ids[:, None])
    rank_ids = jnp.sum(earlier.astype(jnp.int32), axis=1)
    target = owner_ids * capacity + rank_ids
    positions = jnp.arange(group_size * capacity, dtype=jnp.int32)
    matched = target[None, :] == positions[:, None]
    filled = jnp.any(matched, axis=1)
    source = jnp.sum(jnp.where(matched, slot_ids[None, :], 0), axis=1)
    owner_hit = jnp.arange(group_size, dtype=jnp.int32) == my_index
    my_count = jnp.sum(jnp.where(owner_hit, counts, 0))
    my_start = jnp.sum(jnp.where(owner_hit, starts, 0))
    segment = jnp.arange(OWN_SEG, dtype=jnp.int32)
    is_live = segment < my_count
    holder = (my_start + segment) // 2 % group_size
    before = (
        (segment[None, :] < segment[:, None])
        & (holder[None, :] == holder[:, None])
        & is_live[None, :]
    )
    holder_rank = jnp.sum(before.astype(jnp.int32), axis=1)
    row_index = jnp.where(is_live, holder * capacity + holder_rank, 0)
    held_segments = input_grad.reshape(HOLD, SEG, D)
    zero_bf = jnp.zeros((), jnp.bfloat16)
    send_rows = jnp.where(filled[:, None, None], jnp.take(held_segments, source, axis=0), zero_bf)
    received = lax.all_to_all(
        send_rows.reshape(group_size, capacity, SEG, D),
        "fsdp",
        split_axis=0,
        concat_axis=0,
        tiled=True,
    )
    picked = jnp.take(received.reshape(group_size * capacity, SEG, D), row_index, axis=0)
    frames = jnp.where(is_live[:, None, None], picked, zero_bf).reshape(OWN_SEG * SEG, D)
    tap_terms = stem_taps(frames, stem_gathered)
    shifted = jnp.concatenate(
        [tap_terms[0][1:], jnp.zeros((1, tap_terms.shape[2]), jnp.float32)], 0
    )
    odd_rows = tap_terms[2] + shifted
    stem_rows = (
        jnp.stack([tap_terms[1], odd_rows], 1)
        .reshape(2 * OWN_SEG * SEG, tap_terms.shape[2])
        .astype(jnp.bfloat16)
    )
    shard_sum = y_site_sum(z_total).transpose(1, 0, 2).reshape(rows_out, D)
    weight_grad = shard_sum / math.sqrt(lax.axis_size("site") * group_size * HOLD * SEG)
    return (stem_rows[None], weight_grad)


def solution(mesh):
    placed = (
        P("site", "fsdp", None),
        P("site", "fsdp", None),
        P("fsdp", None),
        P(None, "fsdp", None),
        P("site", None),
    )
    return jax.shard_map(
        body,
        mesh=mesh,
        in_specs=placed,
        out_specs=(P("site", "fsdp", None), P("fsdp", None)),
        check_vma=False,
    )
```

```python
import functools
import math

import jax
import jax.numpy as jnp
from jax import lax
from jax.experimental import pallas as pl
from jax.experimental.pallas import tpu as pltpu
from jax.sharding import PartitionSpec as P

D = 1536
SEG = 8
HOLD = 64
OWN_SEG = 128
N_Z = 8


EPSILON = 1e-05


def stem_taps(frames, stem_gathered):
    devices, taps_n, chans = stem_gathered.shape[:3]
    weights = stem_gathered.transpose(1, 0, 2, 3).reshape(taps_n, devices * chans, D)
    return jnp.einsum("rd,kcd->krc", frames, weights, preferred_element_type=jnp.float32)


def ring_pass(n, lanes, prepare=None):
    mesh_kind = pl.DeviceIdType.MESH
    pending = [[None, None] for _ in lanes]
    for step in range(n):
        slot, prev = step % 2, (step + 1) % 2
        sources = []
        for lane_index, lane in enumerate(lanes):
            left, right, chunk_of, land, recv_buf, send_buf, recv_sems, send_sems, free_sem = lane
            if prepare is not None:
                prepare(lane_index, step)
            if step == 0:
                sources.append(chunk_of(step))
                continue
            pltpu.make_async_remote_copy(
                src_ref=send_buf.at[prev],
                dst_ref=recv_buf.at[prev],
                send_sem=send_sems.at[prev],
                recv_sem=recv_sems.at[prev],
                device_id=left,
                device_id_type=mesh_kind,
            ).wait_recv()
            if step < n - 1 and pending[lane_index][slot] is not None:
                pending[lane_index][slot].wait_send()
                pending[lane_index][slot] = None
            target = land if step == n - 1 else send_buf.at[slot]
            target[...] = recv_buf[prev] + chunk_of(step)[...]
            if step <= n - 3:
                pl.semaphore_signal(free_sem, inc=1, device_id=left, device_id_type=mesh_kind)
            sources.append(send_buf.at[slot])
        if step == n - 1:
            break
        for lane_index, (lane, source) in enumerate(zip(lanes, sources)):
            left, right, chunk_of, land, recv_buf, send_buf, recv_sems, send_sems, free_sem = lane
            if step >= 2:
                pl.semaphore_wait(free_sem, 1)
            copy = pltpu.make_async_remote_copy(
                src_ref=source,
                dst_ref=recv_buf.at[slot],
                send_sem=send_sems.at[slot],
                recv_sem=recv_sems.at[slot],
                device_id=right,
                device_id_type=mesh_kind,
            )
            copy.start()
            pending[lane_index][slot] = copy
    for slots in pending:
        for copy in slots:
            if copy is not None:
                copy.wait_send()


def z_sum_kernel(n_z, n_y, lo_ref, hi_ref, ztot, xbuf, zrecv, zsend, swap_sems, dsems, free_sems):
    me = lax.axis_index("fsdp")
    site = lax.axis_index("site")
    core = lax.rem(me, 2)
    chip = me // 2
    zc, yc = chip // n_y, lax.rem(chip, n_y)
    sibling = me + 1 - 2 * core

    def device(z):
        return (site, 2 * (lax.rem(z + n_z, n_z) * n_y + yc) + core)

    mesh_kind = pl.DeviceIdType.MESH
    barrier = pltpu.get_barrier_semaphore()
    peers = ((site, sibling), device(zc - 1), device(zc + 1))
    for peer in peers:
        pl.semaphore_signal(barrier, inc=1, device_id=peer, device_id_type=mesh_kind)
    pl.semaphore_wait(barrier, len(peers))
    ways = (1, -1)
    parts = (lo_ref, hi_ref)

    def rows(lane, step):
        column = lax.rem(zc - ways[lane] * (1 + step) + 2 * n_z, n_z)
        return pl.ds(column * n_y, n_y)

    def swap(lane, step):
        return pltpu.make_async_remote_copy(
            src_ref=parts[lane].at[1 - core, rows(lane, step)],
            dst_ref=xbuf.at[rows(lane, step), lane],
            send_sem=swap_sems.at[lane, step, 0],
            recv_sem=swap_sems.at[lane, step, 1],
            device_id=(site, sibling),
            device_id_type=mesh_kind,
        )

    for step in range(n_z):
        for lane in range(2):
            swap(lane, step).start()

    def prepare(lane, step):
        swap(lane, step).wait_recv()
        here = rows(lane, step)
        xbuf[here, lane] = xbuf[here, lane] + parts[lane][core, here]

    lanes = []
    for lane, way in enumerate(ways):

        def z_chunk(step, lane=lane):
            return xbuf.at[rows(lane, step), lane]

        lanes.append((
            device(zc - way), device(zc + way), z_chunk, ztot.at[:, lane],
            zrecv.at[lane], zsend.at[lane], dsems.at[lane, 0], dsems.at[lane, 1], free_sems.at[lane],
        ))
    ring_pass(n_z, lanes, prepare)
    for step in range(n_z):
        for lane in range(2):
            swap(lane, step).wait_send()


def y_site_kernel(n_y, n_site, ztot, out_ref, yrecv, ysend, ytot, slots, dsems, free_sems, site_send, site_recv):
    me = lax.axis_index("fsdp")
    site = lax.axis_index("site")
    core = lax.rem(me, 2)
    chip = me // 2
    zc, yc = chip // n_y, lax.rem(chip, n_y)

    def device(y):
        return (site, 2 * (zc * n_y + lax.rem(y + n_y, n_y)) + core)

    mesh_kind = pl.DeviceIdType.MESH
    barrier = pltpu.get_barrier_semaphore()
    peers = [device(yc - 1), device(yc + 1)]
    for step in range(1, n_site):
        peers.append((lax.rem(site + step, n_site), me))
    for peer in peers:
        pl.semaphore_signal(barrier, inc=1, device_id=peer, device_id_type=mesh_kind)
    pl.semaphore_wait(barrier, len(peers))
    lanes = []
    for lane, way in enumerate((1, -1)):

        def y_chunk(step, lane=lane, way=way):
            return ztot.at[lax.rem(yc - way * (1 + step) + 2 * n_y, n_y), lane]

        lanes.append((
            device(yc - way), device(yc + way), y_chunk, ytot.at[lane],
            yrecv.at[lane], ysend.at[lane], dsems.at[lane, 0], dsems.at[lane, 1], free_sems.at[lane],
        ))
    ring_pass(n_y, lanes)
    copies = []
    for step in range(1, n_site):
        peer = lax.rem(site + step, n_site)
        copy = pltpu.make_async_remote_copy(
            src_ref=ytot,
            dst_ref=slots.at[site],
            send_sem=site_send.at[step],
            recv_sem=site_recv.at[site],
            device_id=(peer, me),
            device_id_type=mesh_kind,
        )
        copy.start()
        copies.append(copy)
    slots[site] = ytot[...]
    for copy in copies:
        copy.wait_send()
    for step in range(1, n_site):
        src = lax.rem(site + step, n_site)
        pltpu.make_async_remote_copy(
            src_ref=ytot,
            dst_ref=slots.at[src],
            send_sem=site_send.at[0],
            recv_sem=site_recv.at[src],
            device_id=(src, me),
            device_id_type=mesh_kind,
        ).wait_recv()
    total = slots[0]
    for index in range(1, n_site):
        total = total + slots[index]
    out_ref[...] = total


def z_sum(lo, hi, n_z):
    n_chip = lo.shape[1]
    n_y = n_chip // n_z
    lane_block = lo.shape[2:]
    block = (2,) + lane_block
    return pl.pallas_call(
        functools.partial(z_sum_kernel, n_z, n_y),
        out_shape=jax.ShapeDtypeStruct((n_y,) + block, lo.dtype),
        in_specs=[pl.BlockSpec(memory_space=pltpu.VMEM)] * 2,
        out_specs=pl.BlockSpec(memory_space=pltpu.VMEM),
        scratch_shapes=[
            pltpu.VMEM((n_chip,) + block, lo.dtype),
            pltpu.VMEM((2, 2, n_y) + lane_block, lo.dtype),
            pltpu.VMEM((2, 2, n_y) + lane_block, lo.dtype),
            pltpu.SemaphoreType.DMA((2, n_z, 2)),
            pltpu.SemaphoreType.DMA((2, 2, 2)),
            pltpu.SemaphoreType.REGULAR((2,)),
        ],
        compiler_params=pltpu.CompilerParams(collective_id=1, has_side_effects=True),
    )(lo, hi)


def y_site_sum(ztot):
    n_y = ztot.shape[0]
    n_site = lax.axis_size("site")
    block = ztot.shape[1:]
    lane_block = ztot.shape[2:]
    return pl.pallas_call(
        functools.partial(y_site_kernel, n_y, n_site),
        out_shape=jax.ShapeDtypeStruct(block, ztot.dtype),
        in_specs=[pl.BlockSpec(memory_space=pltpu.VMEM)],
        out_specs=pl.BlockSpec(memory_space=pltpu.VMEM),
        scratch_shapes=[
            pltpu.VMEM((2, 2) + lane_block, ztot.dtype),
            pltpu.VMEM((2, 2) + lane_block, ztot.dtype),
            pltpu.VMEM(block, ztot.dtype),
            pltpu.VMEM((n_site,) + block, ztot.dtype),
            pltpu.SemaphoreType.DMA((2, 2, 2)),
            pltpu.SemaphoreType.REGULAR((2,)),
            pltpu.SemaphoreType.DMA((n_site,)),
            pltpu.SemaphoreType.DMA((n_site,)),
        ],
        compiler_params=pltpu.CompilerParams(collective_id=2, has_side_effects=True),
    )(ztot)


def body(held_input, held_cotangent, proj_weight, stem_weight, seg_counts):
    group_size = lax.axis_size("fsdp")
    capacity = 2 * ((OWN_SEG + 2 * group_size - 1) // (2 * group_size))
    my_index = lax.axis_index("fsdp")
    inputs = held_input[0].astype(jnp.float32)
    cotangent = held_cotangent[0]
    row_mean = jnp.mean(inputs, axis=-1, keepdims=True)
    centered = inputs - row_mean
    variance = jnp.mean(centered * centered, axis=-1, keepdims=True)
    inverse = lax.rsqrt(variance + EPSILON)
    normed = centered * inverse
    normed_bf = normed.astype(jnp.bfloat16)
    rows_w = proj_weight.shape[0]
    taps_n, chans = stem_weight.shape[0], stem_weight.shape[1]
    joined = jnp.concatenate([proj_weight, stem_weight.reshape(taps_n * chans, D)], 0)
    gathered = lax.all_gather(joined, "fsdp", axis=0, tiled=False)
    rows_out = D // group_size
    by_core = normed_bf.reshape(normed_bf.shape[0], group_size // 2, 2, rows_out)
    halves = [
        jnp.einsum("rckj,rd->kcjd", by_core, cotangent[:, part * (D // 2):(part + 1) * (D // 2)],
                   preferred_element_type=jnp.float32)
        for part in range(2)
    ]
    z_total = z_sum(halves[0], halves[1], N_Z)
    z_total, gathered = lax.optimization_barrier((z_total, gathered))
    full_weight = gathered[:, :rows_w].reshape(group_size * rows_w, D)
    stem_gathered = gathered[:, rows_w:].reshape(group_size, taps_n, chans, D)
    proj_back = lax.dot_general(
        cotangent,
        full_weight,
        (((1,), (1,)), ((), ())),
        preferred_element_type=jnp.float32,
    )
    input_grad = cotangent.astype(jnp.float32) + inverse * (
        proj_back
        - jnp.mean(proj_back, axis=-1, keepdims=True)
        - normed * jnp.mean(proj_back * normed, axis=-1, keepdims=True)
    )
    input_grad = input_grad.astype(jnp.bfloat16)
    counts = seg_counts[0]
    endings = jnp.cumsum(counts)
    starts = endings - counts
    slot_ids = jnp.arange(HOLD, dtype=jnp.int32)
    item_index = 2 * (slot_ids // 2 * group_size + my_index) + slot_ids % 2
    owner_ids = jnp.sum((item_index[:, None] >= endings[None, :]).astype(jnp.int32), axis=1)
    earlier = (slot_ids[None, :] < slot_ids[:, None]) & (owner_ids[None, :] == owner_ids[:, None])
    rank_ids = jnp.sum(earlier.astype(jnp.int32), axis=1)
    target = owner_ids * capacity + rank_ids
    positions = jnp.arange(group_size * capacity, dtype=jnp.int32)
    matched = target[None, :] == positions[:, None]
    filled = jnp.any(matched, axis=1)
    source = jnp.sum(jnp.where(matched, slot_ids[None, :], 0), axis=1)
    owner_hit = jnp.arange(group_size, dtype=jnp.int32) == my_index
    my_count = jnp.sum(jnp.where(owner_hit, counts, 0))
    my_start = jnp.sum(jnp.where(owner_hit, starts, 0))
    segment = jnp.arange(OWN_SEG, dtype=jnp.int32)
    is_live = segment < my_count
    holder = (my_start + segment) // 2 % group_size
    before = (
        (segment[None, :] < segment[:, None])
        & (holder[None, :] == holder[:, None])
        & is_live[None, :]
    )
    holder_rank = jnp.sum(before.astype(jnp.int32), axis=1)
    row_index = jnp.where(is_live, holder * capacity + holder_rank, 0)
    held_segments = input_grad.reshape(HOLD, SEG, D)
    zero_bf = jnp.zeros((), jnp.bfloat16)
    send_rows = jnp.where(filled[:, None, None], jnp.take(held_segments, source, axis=0), zero_bf)
    received = lax.all_to_all(
        send_rows.reshape(group_size, capacity, SEG, D),
        "fsdp",
        split_axis=0,
        concat_axis=0,
        tiled=True,
    )
    picked = jnp.take(received.reshape(group_size * capacity, SEG, D), row_index, axis=0)
    frames = jnp.where(is_live[:, None, None], picked, zero_bf).reshape(OWN_SEG * SEG, D)
    tap_terms = stem_taps(frames, stem_gathered)
    shifted = jnp.concatenate(
        [tap_terms[0][1:], jnp.zeros((1, tap_terms.shape[2]), jnp.float32)], 0
    )
    odd_rows = tap_terms[2] + shifted
    stem_rows = (
        jnp.stack([tap_terms[1], odd_rows], 1)
        .reshape(2 * OWN_SEG * SEG, tap_terms.shape[2])
        .astype(jnp.bfloat16)
    )
    shard_sum = y_site_sum(z_total).transpose(1, 0, 2).reshape(rows_out, D)
    weight_grad = shard_sum / math.sqrt(lax.axis_size("site") * group_size * HOLD * SEG)
    return (stem_rows[None], weight_grad)


def solution(mesh):
    placed = (
        P("site", "fsdp", None),
        P("site", "fsdp", None),
        P("fsdp", None),
        P(None, "fsdp", None),
        P("site", None),
    )
    return jax.shard_map(
        body,
        mesh=mesh,
        in_specs=placed,
        out_specs=(P("site", "fsdp", None), P("fsdp", None)),
        check_vma=False,
    )
```

```python
import functools
import math

import jax
import jax.numpy as jnp
from jax import lax
from jax.experimental import pallas as pl
from jax.experimental.pallas import tpu as pltpu
from jax.sharding import PartitionSpec as P

D = 1536
SEG = 8
HOLD = 64
OWN_SEG = 128
N_Z = 8
N_LANES = 4


EPSILON = 1e-05


def stem_taps(frames, stem_gathered):
    taps = jnp.einsum(
        "rd,fkcd->krfc", frames, stem_gathered, preferred_element_type=jnp.float32
    )
    return taps.reshape(taps.shape[0], taps.shape[1], -1)


def ring_pass(n, lanes, prepare=None):
    mesh_kind = pl.DeviceIdType.MESH
    for step in range(n):
        slot, prev = step % 2, (step + 1) % 2
        sources = []
        for lane_index, lane in enumerate(lanes):
            left, right, chunk_of, land, recv_buf, send_buf, recv_sems, send_sems, free_sem = lane
            if prepare is not None:
                prepare(lane_index, step)
            if step == 0:
                sources.append(chunk_of(step))
                continue
            pltpu.make_async_remote_copy(
                src_ref=send_buf.at[prev],
                dst_ref=recv_buf.at[prev],
                send_sem=send_sems.at[prev],
                recv_sem=recv_sems.at[prev],
                device_id=left,
                device_id_type=mesh_kind,
            ).wait_recv()
            target = land if step == n - 1 else send_buf.at[slot]
            target[...] = recv_buf[prev] + chunk_of(step)[...]
            if step <= n - 3:
                pl.semaphore_signal(free_sem, inc=1, device_id=left, device_id_type=mesh_kind)
            sources.append(send_buf.at[slot])
        if step == n - 1:
            break
        copies = []
        for lane, source in zip(lanes, sources):
            left, right, chunk_of, land, recv_buf, send_buf, recv_sems, send_sems, free_sem = lane
            if step >= 2:
                pl.semaphore_wait(free_sem, 1)
            copy = pltpu.make_async_remote_copy(
                src_ref=source,
                dst_ref=recv_buf.at[slot],
                send_sem=send_sems.at[slot],
                recv_sem=recv_sems.at[slot],
                device_id=right,
                device_id_type=mesh_kind,
            )
            copy.start()
            copies.append(copy)
        for copy in copies:
            copy.wait_send()


def z_sum_kernel(n_z, n_y, n_lanes, *refs):
    parts = refs[:n_lanes]
    ztot, xbuf, zrecv, zsend, swap_sems, dsems, free_sems = refs[n_lanes:]
    me = lax.axis_index("fsdp")
    site = lax.axis_index("site")
    core = lax.rem(me, 2)
    chip = me // 2
    zc, yc = chip // n_y, lax.rem(chip, n_y)
    sibling = me + 1 - 2 * core

    def device(z):
        return (site, 2 * (lax.rem(z + n_z, n_z) * n_y + yc) + core)

    mesh_kind = pl.DeviceIdType.MESH
    barrier = pltpu.get_barrier_semaphore()
    peers = ((site, sibling), device(zc - 1), device(zc + 1))
    for peer in peers:
        pl.semaphore_signal(barrier, inc=1, device_id=peer, device_id_type=mesh_kind)
    pl.semaphore_wait(barrier, len(peers))
    ways = tuple(1 - 2 * (lane % 2) for lane in range(n_lanes))

    def rows(lane, step):
        column = lax.rem(zc - ways[lane] * (1 + step) + 2 * n_z, n_z)
        return pl.ds(column * n_y, n_y)

    def swap(lane, step):
        return pltpu.make_async_remote_copy(
            src_ref=parts[lane].at[1 - core, rows(lane, step)],
            dst_ref=xbuf.at[rows(lane, step), lane],
            send_sem=swap_sems.at[lane, step, 0],
            recv_sem=swap_sems.at[lane, step, 1],
            device_id=(site, sibling),
            device_id_type=mesh_kind,
        )

    for step in range(n_z):
        for lane in range(n_lanes):
            swap(lane, step).start()

    def prepare(lane, step):
        swap(lane, step).wait_recv()
        here = rows(lane, step)
        xbuf[here, lane] = xbuf[here, lane] + parts[lane][core, here]

    lanes = []
    for lane, way in enumerate(ways):

        def z_chunk(step, lane=lane):
            return xbuf.at[rows(lane, step), lane]

        lanes.append((
            device(zc - way), device(zc + way), z_chunk, ztot.at[:, lane],
            zrecv.at[lane], zsend.at[lane], dsems.at[lane, 0], dsems.at[lane, 1], free_sems.at[lane],
        ))
    ring_pass(n_z, lanes, prepare)
    for step in range(n_z):
        for lane in range(n_lanes):
            swap(lane, step).wait_send()


def y_site_kernel(n_y, n_site, ztot, out_ref, yrecv, ysend, ytot, slots, dsems, free_sems, site_send, site_recv):
    me = lax.axis_index("fsdp")
    site = lax.axis_index("site")
    core = lax.rem(me, 2)
    chip = me // 2
    zc, yc = chip // n_y, lax.rem(chip, n_y)

    def device(y):
        return (site, 2 * (zc * n_y + lax.rem(y + n_y, n_y)) + core)

    mesh_kind = pl.DeviceIdType.MESH
    barrier = pltpu.get_barrier_semaphore()
    peers = [device(yc - 1), device(yc + 1)]
    for step in range(1, n_site):
        peers.append((lax.rem(site + step, n_site), me))
    for peer in peers:
        pl.semaphore_signal(barrier, inc=1, device_id=peer, device_id_type=mesh_kind)
    pl.semaphore_wait(barrier, len(peers))
    lanes = []
    for lane in range(ztot.shape[1]):
        way = 1 - 2 * (lane % 2)

        def y_chunk(step, lane=lane, way=way):
            return ztot.at[lax.rem(yc - way * (1 + step) + 2 * n_y, n_y), lane]

        lanes.append((
            device(yc - way), device(yc + way), y_chunk, ytot.at[lane],
            yrecv.at[lane], ysend.at[lane], dsems.at[lane, 0], dsems.at[lane, 1], free_sems.at[lane],
        ))
    ring_pass(n_y, lanes)
    copies = []
    for step in range(1, n_site):
        peer = lax.rem(site + step, n_site)
        copy = pltpu.make_async_remote_copy(
            src_ref=ytot,
            dst_ref=slots.at[site],
            send_sem=site_send.at[step],
            recv_sem=site_recv.at[site],
            device_id=(peer, me),
            device_id_type=mesh_kind,
        )
        copy.start()
        copies.append(copy)
    slots[site] = ytot[...]
    for copy in copies:
        copy.wait_send()
    for step in range(1, n_site):
        src = lax.rem(site + step, n_site)
        pltpu.make_async_remote_copy(
            src_ref=ytot,
            dst_ref=slots.at[src],
            send_sem=site_send.at[0],
            recv_sem=site_recv.at[src],
            device_id=(src, me),
            device_id_type=mesh_kind,
        ).wait_recv()
    total = slots[0]
    for index in range(1, n_site):
        total = total + slots[index]
    out_ref[...] = total


def z_sum(parts, n_z):
    n_lanes = len(parts)
    n_chip = parts[0].shape[1]
    n_y = n_chip // n_z
    lane_block = parts[0].shape[2:]
    block = (n_lanes,) + lane_block
    dtype = parts[0].dtype
    return pl.pallas_call(
        functools.partial(z_sum_kernel, n_z, n_y, n_lanes),
        out_shape=jax.ShapeDtypeStruct((n_y,) + block, dtype),
        in_specs=[pl.BlockSpec(memory_space=pltpu.VMEM)] * n_lanes,
        out_specs=pl.BlockSpec(memory_space=pltpu.VMEM),
        scratch_shapes=[
            pltpu.VMEM((n_chip,) + block, dtype),
            pltpu.VMEM((n_lanes, 2, n_y) + lane_block, dtype),
            pltpu.VMEM((n_lanes, 2, n_y) + lane_block, dtype),
            pltpu.SemaphoreType.DMA((n_lanes, n_z, 2)),
            pltpu.SemaphoreType.DMA((n_lanes, 2, 2)),
            pltpu.SemaphoreType.REGULAR((n_lanes,)),
        ],
        compiler_params=pltpu.CompilerParams(collective_id=1, has_side_effects=True),
    )(*parts)


def y_site_sum(ztot):
    n_y = ztot.shape[0]
    n_site = lax.axis_size("site")
    block = ztot.shape[1:]
    lane_block = ztot.shape[2:]
    n_lanes = ztot.shape[1]
    return pl.pallas_call(
        functools.partial(y_site_kernel, n_y, n_site),
        out_shape=jax.ShapeDtypeStruct(block, ztot.dtype),
        in_specs=[pl.BlockSpec(memory_space=pltpu.VMEM)],
        out_specs=pl.BlockSpec(memory_space=pltpu.VMEM),
        scratch_shapes=[
            pltpu.VMEM((n_lanes, 2) + lane_block, ztot.dtype),
            pltpu.VMEM((n_lanes, 2) + lane_block, ztot.dtype),
            pltpu.VMEM(block, ztot.dtype),
            pltpu.VMEM((n_site,) + block, ztot.dtype),
            pltpu.SemaphoreType.DMA((n_lanes, 2, 2)),
            pltpu.SemaphoreType.REGULAR((n_lanes,)),
            pltpu.SemaphoreType.DMA((n_site,)),
            pltpu.SemaphoreType.DMA((n_site,)),
        ],
        compiler_params=pltpu.CompilerParams(collective_id=2, has_side_effects=True),
    )(ztot)


def body(held_input, held_cotangent, proj_weight, stem_weight, seg_counts):
    group_size = lax.axis_size("fsdp")
    capacity = 2 * ((OWN_SEG + 2 * group_size - 1) // (2 * group_size))
    my_index = lax.axis_index("fsdp")
    inputs = held_input[0].astype(jnp.float32)
    cotangent = held_cotangent[0]
    row_mean = jnp.mean(inputs, axis=-1, keepdims=True)
    centered = inputs - row_mean
    variance = jnp.mean(centered * centered, axis=-1, keepdims=True)
    inverse = lax.rsqrt(variance + EPSILON)
    normed = centered * inverse
    normed_bf = normed.astype(jnp.bfloat16)
    rows_w = proj_weight.shape[0]
    taps_n, chans = stem_weight.shape[0], stem_weight.shape[1]
    joined = jnp.concatenate([proj_weight, stem_weight.reshape(taps_n * chans, D)], 0)
    gathered = lax.all_gather(joined, "fsdp", axis=0, tiled=False)
    rows_out = D // group_size
    by_core = normed_bf.reshape(normed_bf.shape[0], group_size // 2, 2, rows_out)
    width = D // N_LANES
    pieces = [
        jnp.einsum("rckj,rd->kcjd", by_core, cotangent[:, part * width:(part + 1) * width],
                   preferred_element_type=jnp.float32)
        for part in range(N_LANES)
    ]
    z_total = z_sum(pieces, N_Z)
    z_total, gathered = lax.optimization_barrier((z_total, gathered))
    full_weight = gathered[:, :rows_w].reshape(group_size * rows_w, D)
    stem_gathered = gathered[:, rows_w:].reshape(group_size, taps_n, chans, D)
    proj_back = lax.dot_general(
        cotangent,
        full_weight,
        (((1,), (1,)), ((), ())),
        preferred_element_type=jnp.float32,
    )
    input_grad = cotangent.astype(jnp.float32) + inverse * (
        proj_back
        - jnp.mean(proj_back, axis=-1, keepdims=True)
        - normed * jnp.mean(proj_back * normed, axis=-1, keepdims=True)
    )
    input_grad = input_grad.astype(jnp.bfloat16)
    counts = seg_counts[0]
    endings = jnp.cumsum(counts)
    starts = endings - counts
    slot_ids = jnp.arange(HOLD, dtype=jnp.int32)
    item_index = 2 * (slot_ids // 2 * group_size + my_index) + slot_ids % 2
    owner_ids = jnp.sum((item_index[:, None] >= endings[None, :]).astype(jnp.int32), axis=1)
    earlier = (slot_ids[None, :] < slot_ids[:, None]) & (owner_ids[None, :] == owner_ids[:, None])
    rank_ids = jnp.sum(earlier.astype(jnp.int32), axis=1)
    target = owner_ids * capacity + rank_ids
    positions = jnp.arange(group_size * capacity, dtype=jnp.int32)
    matched = target[None, :] == positions[:, None]
    filled = jnp.any(matched, axis=1)
    source = jnp.sum(jnp.where(matched, slot_ids[None, :], 0), axis=1)
    owner_hit = jnp.arange(group_size, dtype=jnp.int32) == my_index
    my_count = jnp.sum(jnp.where(owner_hit, counts, 0))
    my_start = jnp.sum(jnp.where(owner_hit, starts, 0))
    segment = jnp.arange(OWN_SEG, dtype=jnp.int32)
    is_live = segment < my_count
    holder = (my_start + segment) // 2 % group_size
    before = (
        (segment[None, :] < segment[:, None])
        & (holder[None, :] == holder[:, None])
        & is_live[None, :]
    )
    holder_rank = jnp.sum(before.astype(jnp.int32), axis=1)
    row_index = jnp.where(is_live, holder * capacity + holder_rank, 0)
    held_segments = input_grad.reshape(HOLD, SEG, D)
    zero_bf = jnp.zeros((), jnp.bfloat16)
    send_rows = jnp.where(filled[:, None, None], jnp.take(held_segments, source, axis=0), zero_bf)
    received = lax.all_to_all(
        send_rows.reshape(group_size, capacity, SEG, D),
        "fsdp",
        split_axis=0,
        concat_axis=0,
        tiled=True,
    )
    picked = jnp.take(received.reshape(group_size * capacity, SEG, D), row_index, axis=0)
    frames = jnp.where(is_live[:, None, None], picked, zero_bf).reshape(OWN_SEG * SEG, D)
    tap_terms = stem_taps(frames, stem_gathered)
    shifted = jnp.concatenate(
        [tap_terms[0][1:], jnp.zeros((1, tap_terms.shape[2]), jnp.float32)], 0
    )
    odd_rows = tap_terms[2] + shifted
    stem_rows = (
        jnp.stack([tap_terms[1], odd_rows], 1)
        .reshape(2 * OWN_SEG * SEG, tap_terms.shape[2])
        .astype(jnp.bfloat16)
    )
    shard_sum = y_site_sum(z_total).transpose(1, 0, 2).reshape(rows_out, D)
    weight_grad = shard_sum / math.sqrt(lax.axis_size("site") * group_size * HOLD * SEG)
    return (stem_rows[None], weight_grad)


def solution(mesh):
    placed = (
        P("site", "fsdp", None),
        P("site", "fsdp", None),
        P("fsdp", None),
        P(None, "fsdp", None),
        P("site", None),
    )
    return jax.shard_map(
        body,
        mesh=mesh,
        in_specs=placed,
        out_specs=(P("site", "fsdp", None), P("fsdp", None)),
        check_vma=False,
    )
```

```python
import functools
import math

import jax
import jax.numpy as jnp
from jax import lax
from jax.experimental import pallas as pl
from jax.experimental.pallas import tpu as pltpu
from jax.sharding import PartitionSpec as P

D = 1536
SEG = 8
HOLD = 64
OWN_SEG = 128
N_Z = 8


EPSILON = 1e-05


def stem_taps(frames, stem_gathered):
    devices, taps_n, chans = stem_gathered.shape[:3]
    width = devices * chans
    weights = stem_gathered.transpose(1, 0, 2, 3).reshape(taps_n * width, D)
    flat = lax.dot_general(frames, weights, (((1,), (1,)), ((), ())), preferred_element_type=jnp.float32)
    return [flat[:, tap * width:(tap + 1) * width] for tap in range(taps_n)]


def ring_pass(n, lanes, prepare=None):
    mesh_kind = pl.DeviceIdType.MESH
    for step in range(n):
        slot, prev = step % 2, (step + 1) % 2
        sources = []
        for lane_index, lane in enumerate(lanes):
            left, right, chunk_of, land, recv_buf, send_buf, recv_sems, send_sems, free_sem = lane
            if prepare is not None:
                prepare(lane_index, step)
            if step == 0:
                sources.append(chunk_of(step))
                continue
            pltpu.make_async_remote_copy(
                src_ref=send_buf.at[prev],
                dst_ref=recv_buf.at[prev],
                send_sem=send_sems.at[prev],
                recv_sem=recv_sems.at[prev],
                device_id=left,
                device_id_type=mesh_kind,
            ).wait_recv()
            target = land if step == n - 1 else send_buf.at[slot]
            target[...] = recv_buf[prev] + chunk_of(step)[...]
            if step <= n - 3:
                pl.semaphore_signal(free_sem, inc=1, device_id=left, device_id_type=mesh_kind)
            sources.append(send_buf.at[slot])
        if step == n - 1:
            break
        copies = []
        for lane, source in zip(lanes, sources):
            left, right, chunk_of, land, recv_buf, send_buf, recv_sems, send_sems, free_sem = lane
            if step >= 2:
                pl.semaphore_wait(free_sem, 1)
            copy = pltpu.make_async_remote_copy(
                src_ref=source,
                dst_ref=recv_buf.at[slot],
                send_sem=send_sems.at[slot],
                recv_sem=recv_sems.at[slot],
                device_id=right,
                device_id_type=mesh_kind,
            )
            copy.start()
            copies.append(copy)
        for copy in copies:
            copy.wait_send()


def z_sum_kernel(n_z, n_y, lo_ref, hi_ref, ztot, xbuf, zrecv, zsend, swap_sems, dsems, free_sems):
    me = lax.axis_index("fsdp")
    site = lax.axis_index("site")
    core = lax.rem(me, 2)
    chip = me // 2
    zc, yc = chip // n_y, lax.rem(chip, n_y)
    sibling = me + 1 - 2 * core

    def device(z):
        return (site, 2 * (lax.rem(z + n_z, n_z) * n_y + yc) + core)

    mesh_kind = pl.DeviceIdType.MESH
    barrier = pltpu.get_barrier_semaphore()
    peers = ((site, sibling), device(zc - 1), device(zc + 1))
    for peer in peers:
        pl.semaphore_signal(barrier, inc=1, device_id=peer, device_id_type=mesh_kind)
    pl.semaphore_wait(barrier, len(peers))
    ways = (1, -1)
    parts = (lo_ref, hi_ref)

    def rows(lane, step):
        column = lax.rem(zc - ways[lane] * (1 + step) + 2 * n_z, n_z)
        return pl.ds(column * n_y, n_y)

    def swap(lane, step):
        return pltpu.make_async_remote_copy(
            src_ref=parts[lane].at[1 - core, rows(lane, step)],
            dst_ref=xbuf.at[rows(lane, step), lane],
            send_sem=swap_sems.at[lane, step, 0],
            recv_sem=swap_sems.at[lane, step, 1],
            device_id=(site, sibling),
            device_id_type=mesh_kind,
        )

    for step in range(n_z):
        for lane in range(2):
            swap(lane, step).start()

    def prepare(lane, step):
        swap(lane, step).wait_recv()
        here = rows(lane, step)
        xbuf[here, lane] = xbuf[here, lane] + parts[lane][core, here]

    lanes = []
    for lane, way in enumerate(ways):

        def z_chunk(step, lane=lane):
            return xbuf.at[rows(lane, step), lane]

        lanes.append((
            device(zc - way), device(zc + way), z_chunk, ztot.at[:, lane],
            zrecv.at[lane], zsend.at[lane], dsems.at[lane, 0], dsems.at[lane, 1], free_sems.at[lane],
        ))
    ring_pass(n_z, lanes, prepare)
    for step in range(n_z):
        for lane in range(2):
            swap(lane, step).wait_send()


def y_site_kernel(n_y, n_site, ztot, out_ref, yrecv, ysend, ytot, slots, dsems, free_sems, site_send, site_recv):
    me = lax.axis_index("fsdp")
    site = lax.axis_index("site")
    core = lax.rem(me, 2)
    chip = me // 2
    zc, yc = chip // n_y, lax.rem(chip, n_y)

    def device(y):
        return (site, 2 * (zc * n_y + lax.rem(y + n_y, n_y)) + core)

    mesh_kind = pl.DeviceIdType.MESH
    barrier = pltpu.get_barrier_semaphore()
    peers = [device(yc - 1), device(yc + 1)]
    for step in range(1, n_site):
        peers.append((lax.rem(site + step, n_site), me))
    for peer in peers:
        pl.semaphore_signal(barrier, inc=1, device_id=peer, device_id_type=mesh_kind)
    pl.semaphore_wait(barrier, len(peers))
    lanes = []
    for lane, way in enumerate((1, -1)):

        def y_chunk(step, lane=lane, way=way):
            return ztot.at[lax.rem(yc - way * (1 + step) + 2 * n_y, n_y), lane]

        lanes.append((
            device(yc - way), device(yc + way), y_chunk, ytot.at[lane],
            yrecv.at[lane], ysend.at[lane], dsems.at[lane, 0], dsems.at[lane, 1], free_sems.at[lane],
        ))
    ring_pass(n_y, lanes)
    copies = []
    for step in range(1, n_site):
        peer = lax.rem(site + step, n_site)
        copy = pltpu.make_async_remote_copy(
            src_ref=ytot,
            dst_ref=slots.at[site],
            send_sem=site_send.at[step],
            recv_sem=site_recv.at[site],
            device_id=(peer, me),
            device_id_type=mesh_kind,
        )
        copy.start()
        copies.append(copy)
    slots[site] = ytot[...]
    for copy in copies:
        copy.wait_send()
    for step in range(1, n_site):
        src = lax.rem(site + step, n_site)
        pltpu.make_async_remote_copy(
            src_ref=ytot,
            dst_ref=slots.at[src],
            send_sem=site_send.at[0],
            recv_sem=site_recv.at[src],
            device_id=(src, me),
            device_id_type=mesh_kind,
        ).wait_recv()
    total = slots[0]
    for index in range(1, n_site):
        total = total + slots[index]
    out_ref[...] = total


def z_sum(lo, hi, n_z):
    n_chip = lo.shape[1]
    n_y = n_chip // n_z
    lane_block = lo.shape[2:]
    block = (2,) + lane_block
    return pl.pallas_call(
        functools.partial(z_sum_kernel, n_z, n_y),
        out_shape=jax.ShapeDtypeStruct((n_y,) + block, lo.dtype),
        in_specs=[pl.BlockSpec(memory_space=pltpu.VMEM)] * 2,
        out_specs=pl.BlockSpec(memory_space=pltpu.VMEM),
        scratch_shapes=[
            pltpu.VMEM((n_chip,) + block, lo.dtype),
            pltpu.VMEM((2, 2, n_y) + lane_block, lo.dtype),
            pltpu.VMEM((2, 2, n_y) + lane_block, lo.dtype),
            pltpu.SemaphoreType.DMA((2, n_z, 2)),
            pltpu.SemaphoreType.DMA((2, 2, 2)),
            pltpu.SemaphoreType.REGULAR((2,)),
        ],
        compiler_params=pltpu.CompilerParams(collective_id=1, has_side_effects=True),
    )(lo, hi)


def y_site_sum(ztot):
    n_y = ztot.shape[0]
    n_site = lax.axis_size("site")
    block = ztot.shape[1:]
    lane_block = ztot.shape[2:]
    return pl.pallas_call(
        functools.partial(y_site_kernel, n_y, n_site),
        out_shape=jax.ShapeDtypeStruct(block, ztot.dtype),
        in_specs=[pl.BlockSpec(memory_space=pltpu.VMEM)],
        out_specs=pl.BlockSpec(memory_space=pltpu.VMEM),
        scratch_shapes=[
            pltpu.VMEM((2, 2) + lane_block, ztot.dtype),
            pltpu.VMEM((2, 2) + lane_block, ztot.dtype),
            pltpu.VMEM(block, ztot.dtype),
            pltpu.VMEM((n_site,) + block, ztot.dtype),
            pltpu.SemaphoreType.DMA((2, 2, 2)),
            pltpu.SemaphoreType.REGULAR((2,)),
            pltpu.SemaphoreType.DMA((n_site,)),
            pltpu.SemaphoreType.DMA((n_site,)),
        ],
        compiler_params=pltpu.CompilerParams(collective_id=2, has_side_effects=True),
    )(ztot)


def body(held_input, held_cotangent, proj_weight, stem_weight, seg_counts):
    group_size = lax.axis_size("fsdp")
    capacity = 2 * ((OWN_SEG + 2 * group_size - 1) // (2 * group_size))
    my_index = lax.axis_index("fsdp")
    inputs = held_input[0].astype(jnp.float32)
    cotangent = held_cotangent[0]
    row_mean = jnp.mean(inputs, axis=-1, keepdims=True)
    centered = inputs - row_mean
    variance = jnp.mean(centered * centered, axis=-1, keepdims=True)
    inverse = lax.rsqrt(variance + EPSILON)
    normed = centered * inverse
    normed_bf = normed.astype(jnp.bfloat16)
    rows_w = proj_weight.shape[0]
    taps_n, chans = stem_weight.shape[0], stem_weight.shape[1]
    joined = jnp.concatenate([proj_weight, stem_weight.reshape(taps_n * chans, D)], 0)
    gathered = lax.all_gather(joined, "fsdp", axis=0, tiled=False)
    rows_out = D // group_size
    by_core = normed_bf.reshape(normed_bf.shape[0], group_size // 2, 2, rows_out)
    halves = [
        jnp.einsum("rckj,rd->kcjd", by_core, cotangent[:, part * (D // 2):(part + 1) * (D // 2)],
                   preferred_element_type=jnp.float32)
        for part in range(2)
    ]
    z_total = z_sum(halves[0], halves[1], N_Z)
    z_total, gathered = lax.optimization_barrier((z_total, gathered))
    full_weight = gathered[:, :rows_w].reshape(group_size * rows_w, D)
    stem_gathered = gathered[:, rows_w:].reshape(group_size, taps_n, chans, D)
    proj_back = lax.dot_general(
        cotangent,
        full_weight,
        (((1,), (1,)), ((), ())),
        preferred_element_type=jnp.float32,
    )
    input_grad = cotangent.astype(jnp.float32) + inverse * (
        proj_back
        - jnp.mean(proj_back, axis=-1, keepdims=True)
        - normed * jnp.mean(proj_back * normed, axis=-1, keepdims=True)
    )
    input_grad = input_grad.astype(jnp.bfloat16)
    counts = seg_counts[0]
    endings = jnp.cumsum(counts)
    starts = endings - counts
    slot_ids = jnp.arange(HOLD, dtype=jnp.int32)
    item_index = 2 * (slot_ids // 2 * group_size + my_index) + slot_ids % 2
    owner_ids = jnp.sum((item_index[:, None] >= endings[None, :]).astype(jnp.int32), axis=1)
    earlier = (slot_ids[None, :] < slot_ids[:, None]) & (owner_ids[None, :] == owner_ids[:, None])
    rank_ids = jnp.sum(earlier.astype(jnp.int32), axis=1)
    target = owner_ids * capacity + rank_ids
    positions = jnp.arange(group_size * capacity, dtype=jnp.int32)
    matched = target[None, :] == positions[:, None]
    filled = jnp.any(matched, axis=1)
    source = jnp.sum(jnp.where(matched, slot_ids[None, :], 0), axis=1)
    owner_hit = jnp.arange(group_size, dtype=jnp.int32) == my_index
    my_count = jnp.sum(jnp.where(owner_hit, counts, 0))
    my_start = jnp.sum(jnp.where(owner_hit, starts, 0))
    segment = jnp.arange(OWN_SEG, dtype=jnp.int32)
    is_live = segment < my_count
    holder = (my_start + segment) // 2 % group_size
    before = (
        (segment[None, :] < segment[:, None])
        & (holder[None, :] == holder[:, None])
        & is_live[None, :]
    )
    holder_rank = jnp.sum(before.astype(jnp.int32), axis=1)
    row_index = jnp.where(is_live, holder * capacity + holder_rank, 0)
    held_segments = input_grad.reshape(HOLD, SEG, D)
    zero_bf = jnp.zeros((), jnp.bfloat16)
    send_rows = jnp.where(filled[:, None, None], jnp.take(held_segments, source, axis=0), zero_bf)
    received = lax.all_to_all(
        send_rows.reshape(group_size, capacity, SEG, D),
        "fsdp",
        split_axis=0,
        concat_axis=0,
        tiled=True,
    )
    picked = jnp.take(received.reshape(group_size * capacity, SEG, D), row_index, axis=0)
    frames = jnp.where(is_live[:, None, None], picked, zero_bf).reshape(OWN_SEG * SEG, D)
    tap_terms = stem_taps(frames, stem_gathered)
    shifted = jnp.concatenate(
        [tap_terms[0][1:], jnp.zeros((1, tap_terms[0].shape[1]), jnp.float32)], 0
    )
    odd_rows = tap_terms[2] + shifted
    stem_rows = (
        jnp.concatenate([tap_terms[1], odd_rows], 1)
        .astype(jnp.bfloat16)
        .reshape(2 * OWN_SEG * SEG, tap_terms[0].shape[1])
    )
    shard_sum = y_site_sum(z_total).transpose(1, 0, 2).reshape(rows_out, D)
    weight_grad = shard_sum / math.sqrt(lax.axis_size("site") * group_size * HOLD * SEG)
    return (stem_rows[None], weight_grad)


def solution(mesh):
    placed = (
        P("site", "fsdp", None),
        P("site", "fsdp", None),
        P("fsdp", None),
        P(None, "fsdp", None),
        P("site", None),
    )
    return jax.shard_map(
        body,
        mesh=mesh,
        in_specs=placed,
        out_specs=(P("site", "fsdp", None), P("fsdp", None)),
        check_vma=False,
    )
```

```python
import functools
import math

import jax
import jax.numpy as jnp
from jax import lax
from jax.experimental import pallas as pl
from jax.experimental.pallas import tpu as pltpu
from jax.sharding import PartitionSpec as P

D = 1536
SEG = 8
HOLD = 64
OWN_SEG = 128
N_Z = 8


EPSILON = 1e-05


def stem_taps(frames, stem_gathered):
    devices, taps_n, chans = stem_gathered.shape[:3]
    width = devices * chans
    weights = stem_gathered.transpose(1, 0, 2, 3).reshape(taps_n * width, D)
    flat = lax.dot_general(frames, weights, (((1,), (1,)), ((), ())), preferred_element_type=jnp.float32)
    return [flat[:, tap * width:(tap + 1) * width] for tap in range(taps_n)]


def ring_pass(n, lanes, prepare=None):
    mesh_kind = pl.DeviceIdType.MESH
    for step in range(n):
        slot, prev = step % 2, (step + 1) % 2
        sources = []
        for lane_index, lane in enumerate(lanes):
            left, right, chunk_of, land, recv_buf, send_buf, recv_sems, send_sems, free_sem = lane
            if prepare is not None:
                prepare(lane_index, step)
            if step == 0:
                sources.append(chunk_of(step))
                continue
            pltpu.make_async_remote_copy(
                src_ref=send_buf.at[prev],
                dst_ref=recv_buf.at[prev],
                send_sem=send_sems.at[prev],
                recv_sem=recv_sems.at[prev],
                device_id=left,
                device_id_type=mesh_kind,
            ).wait_recv()
            target = land if step == n - 1 else send_buf.at[slot]
            target[...] = recv_buf[prev] + chunk_of(step)[...]
            if step <= n - 3:
                pl.semaphore_signal(free_sem, inc=1, device_id=left, device_id_type=mesh_kind)
            sources.append(send_buf.at[slot])
        if step == n - 1:
            break
        copies = []
        for lane, source in zip(lanes, sources):
            left, right, chunk_of, land, recv_buf, send_buf, recv_sems, send_sems, free_sem = lane
            if step >= 2:
                pl.semaphore_wait(free_sem, 1)
            copy = pltpu.make_async_remote_copy(
                src_ref=source,
                dst_ref=recv_buf.at[slot],
                send_sem=send_sems.at[slot],
                recv_sem=recv_sems.at[slot],
                device_id=right,
                device_id_type=mesh_kind,
            )
            copy.start()
            copies.append(copy)
        for copy in copies:
            copy.wait_send()


def z_sum_kernel(n_z, n_y, lo_ref, hi_ref, ztot, xbuf, zrecv, zsend, swap_sems, dsems, free_sems):
    me = lax.axis_index("fsdp")
    site = lax.axis_index("site")
    core = lax.rem(me, 2)
    chip = me // 2
    zc, yc = chip // n_y, lax.rem(chip, n_y)
    sibling = me + 1 - 2 * core

    def device(z):
        return (site, 2 * (lax.rem(z + n_z, n_z) * n_y + yc) + core)

    mesh_kind = pl.DeviceIdType.MESH
    barrier = pltpu.get_barrier_semaphore()
    peers = ((site, sibling), device(zc - 1), device(zc + 1))
    for peer in peers:
        pl.semaphore_signal(barrier, inc=1, device_id=peer, device_id_type=mesh_kind)
    pl.semaphore_wait(barrier, len(peers))
    ways = (1, -1)
    parts = (lo_ref, hi_ref)

    def rows(lane, step):
        column = lax.rem(zc - ways[lane] * (1 + step) + 2 * n_z, n_z)
        return pl.ds(column * n_y, n_y)

    def swap(lane, step):
        return pltpu.make_async_remote_copy(
            src_ref=parts[lane].at[1 - core, rows(lane, step)],
            dst_ref=xbuf.at[rows(lane, step), lane],
            send_sem=swap_sems.at[lane, step, 0],
            recv_sem=swap_sems.at[lane, step, 1],
            device_id=(site, sibling),
            device_id_type=mesh_kind,
        )

    for step in range(n_z):
        for lane in range(2):
            swap(lane, step).start()

    def prepare(lane, step):
        swap(lane, step).wait_recv()
        here = rows(lane, step)
        xbuf[here, lane] = xbuf[here, lane] + parts[lane][core, here]

    lanes = []
    for lane, way in enumerate(ways):

        def z_chunk(step, lane=lane):
            return xbuf.at[rows(lane, step), lane]

        lanes.append((
            device(zc - way), device(zc + way), z_chunk, ztot.at[:, lane],
            zrecv.at[lane], zsend.at[lane], dsems.at[lane, 0], dsems.at[lane, 1], free_sems.at[lane],
        ))
    ring_pass(n_z, lanes, prepare)
    for step in range(n_z):
        for lane in range(2):
            swap(lane, step).wait_send()


def y_site_kernel(n_y, n_site, ztot, out_ref, yrecv, ysend, ytot, slots, dsems, free_sems, site_send, site_recv):
    me = lax.axis_index("fsdp")
    site = lax.axis_index("site")
    core = lax.rem(me, 2)
    chip = me // 2
    zc, yc = chip // n_y, lax.rem(chip, n_y)

    def device(y):
        return (site, 2 * (zc * n_y + lax.rem(y + n_y, n_y)) + core)

    mesh_kind = pl.DeviceIdType.MESH
    barrier = pltpu.get_barrier_semaphore()
    peers = [device(yc - 1), device(yc + 1)]
    for step in range(1, n_site):
        peers.append((lax.rem(site + step, n_site), me))
    for peer in peers:
        pl.semaphore_signal(barrier, inc=1, device_id=peer, device_id_type=mesh_kind)
    pl.semaphore_wait(barrier, len(peers))
    lanes = []
    for lane, way in enumerate((1, -1)):

        def y_chunk(step, lane=lane, way=way):
            return ztot.at[lax.rem(yc - way * (1 + step) + 2 * n_y, n_y), lane]

        lanes.append((
            device(yc - way), device(yc + way), y_chunk, ytot.at[lane],
            yrecv.at[lane], ysend.at[lane], dsems.at[lane, 0], dsems.at[lane, 1], free_sems.at[lane],
        ))
    ring_pass(n_y, lanes)
    copies = []
    for step in range(1, n_site):
        peer = lax.rem(site + step, n_site)
        copy = pltpu.make_async_remote_copy(
            src_ref=ytot,
            dst_ref=slots.at[site],
            send_sem=site_send.at[step],
            recv_sem=site_recv.at[site],
            device_id=(peer, me),
            device_id_type=mesh_kind,
        )
        copy.start()
        copies.append(copy)
    slots[site] = ytot[...]
    for copy in copies:
        copy.wait_send()
    for step in range(1, n_site):
        src = lax.rem(site + step, n_site)
        pltpu.make_async_remote_copy(
            src_ref=ytot,
            dst_ref=slots.at[src],
            send_sem=site_send.at[0],
            recv_sem=site_recv.at[src],
            device_id=(src, me),
            device_id_type=mesh_kind,
        ).wait_recv()
    total = slots[0]
    for index in range(1, n_site):
        total = total + slots[index]
    out_ref[...] = total


def z_sum(lo, hi, n_z):
    n_chip = lo.shape[1]
    n_y = n_chip // n_z
    lane_block = lo.shape[2:]
    block = (2,) + lane_block
    return pl.pallas_call(
        functools.partial(z_sum_kernel, n_z, n_y),
        out_shape=jax.ShapeDtypeStruct((n_y,) + block, lo.dtype),
        in_specs=[pl.BlockSpec(memory_space=pltpu.VMEM)] * 2,
        out_specs=pl.BlockSpec(memory_space=pltpu.VMEM),
        scratch_shapes=[
            pltpu.VMEM((n_chip,) + block, lo.dtype),
            pltpu.VMEM((2, 2, n_y) + lane_block, lo.dtype),
            pltpu.VMEM((2, 2, n_y) + lane_block, lo.dtype),
            pltpu.SemaphoreType.DMA((2, n_z, 2)),
            pltpu.SemaphoreType.DMA((2, 2, 2)),
            pltpu.SemaphoreType.REGULAR((2,)),
        ],
        compiler_params=pltpu.CompilerParams(collective_id=1, has_side_effects=True),
    )(lo, hi)


def y_site_sum(ztot):
    n_y = ztot.shape[0]
    n_site = lax.axis_size("site")
    block = ztot.shape[1:]
    lane_block = ztot.shape[2:]
    return pl.pallas_call(
        functools.partial(y_site_kernel, n_y, n_site),
        out_shape=jax.ShapeDtypeStruct(block, ztot.dtype),
        in_specs=[pl.BlockSpec(memory_space=pltpu.VMEM)],
        out_specs=pl.BlockSpec(memory_space=pltpu.VMEM),
        scratch_shapes=[
            pltpu.VMEM((2, 2) + lane_block, ztot.dtype),
            pltpu.VMEM((2, 2) + lane_block, ztot.dtype),
            pltpu.VMEM(block, ztot.dtype),
            pltpu.VMEM((n_site,) + block, ztot.dtype),
            pltpu.SemaphoreType.DMA((2, 2, 2)),
            pltpu.SemaphoreType.REGULAR((2,)),
            pltpu.SemaphoreType.DMA((n_site,)),
            pltpu.SemaphoreType.DMA((n_site,)),
        ],
        compiler_params=pltpu.CompilerParams(collective_id=2, has_side_effects=True),
    )(ztot)


def body(held_input, held_cotangent, proj_weight, stem_weight, seg_counts):
    group_size = lax.axis_size("fsdp")
    capacity = 2 * ((OWN_SEG + 2 * group_size - 1) // (2 * group_size))
    my_index = lax.axis_index("fsdp")
    inputs = held_input[0].astype(jnp.float32)
    cotangent = held_cotangent[0]
    row_mean = jnp.mean(inputs, axis=-1, keepdims=True)
    centered = inputs - row_mean
    variance = jnp.mean(centered * centered, axis=-1, keepdims=True)
    inverse = lax.rsqrt(variance + EPSILON)
    normed = centered * inverse
    normed_bf = normed.astype(jnp.bfloat16)
    rows_w = proj_weight.shape[0]
    taps_n, chans = stem_weight.shape[0], stem_weight.shape[1]
    joined = jnp.concatenate([proj_weight, stem_weight.reshape(taps_n * chans, D)], 1)
    gathered = lax.all_gather(joined, "fsdp", axis=0, tiled=True)
    rows_out = D // group_size
    by_core = normed_bf.reshape(normed_bf.shape[0], group_size // 2, 2, rows_out)
    halves = [
        jnp.einsum("rckj,rd->kcjd", by_core, cotangent[:, part * (D // 2):(part + 1) * (D // 2)],
                   preferred_element_type=jnp.float32)
        for part in range(2)
    ]
    z_total = z_sum(halves[0], halves[1], N_Z)
    z_total, gathered = lax.optimization_barrier((z_total, gathered))
    full_weight = gathered[:, :D]
    stem_gathered = gathered[:, D:].reshape(group_size, taps_n, chans, D)
    proj_back = lax.dot_general(
        cotangent,
        full_weight,
        (((1,), (1,)), ((), ())),
        preferred_element_type=jnp.float32,
    )
    input_grad = cotangent.astype(jnp.float32) + inverse * (
        proj_back
        - jnp.mean(proj_back, axis=-1, keepdims=True)
        - normed * jnp.mean(proj_back * normed, axis=-1, keepdims=True)
    )
    input_grad = input_grad.astype(jnp.bfloat16)
    counts = seg_counts[0]
    endings = jnp.cumsum(counts)
    starts = endings - counts
    slot_ids = jnp.arange(HOLD, dtype=jnp.int32)
    item_index = 2 * (slot_ids // 2 * group_size + my_index) + slot_ids % 2
    owner_ids = jnp.sum((item_index[:, None] >= endings[None, :]).astype(jnp.int32), axis=1)
    earlier = (slot_ids[None, :] < slot_ids[:, None]) & (owner_ids[None, :] == owner_ids[:, None])
    rank_ids = jnp.sum(earlier.astype(jnp.int32), axis=1)
    target = owner_ids * capacity + rank_ids
    positions = jnp.arange(group_size * capacity, dtype=jnp.int32)
    matched = target[None, :] == positions[:, None]
    filled = jnp.any(matched, axis=1)
    source = jnp.sum(jnp.where(matched, slot_ids[None, :], 0), axis=1)
    owner_hit = jnp.arange(group_size, dtype=jnp.int32) == my_index
    my_count = jnp.sum(jnp.where(owner_hit, counts, 0))
    my_start = jnp.sum(jnp.where(owner_hit, starts, 0))
    segment = jnp.arange(OWN_SEG, dtype=jnp.int32)
    is_live = segment < my_count
    holder = (my_start + segment) // 2 % group_size
    before = (
        (segment[None, :] < segment[:, None])
        & (holder[None, :] == holder[:, None])
        & is_live[None, :]
    )
    holder_rank = jnp.sum(before.astype(jnp.int32), axis=1)
    row_index = jnp.where(is_live, holder * capacity + holder_rank, 0)
    held_segments = input_grad.reshape(HOLD, SEG, D)
    zero_bf = jnp.zeros((), jnp.bfloat16)
    send_rows = jnp.where(filled[:, None, None], jnp.take(held_segments, source, axis=0), zero_bf)
    received = lax.all_to_all(
        send_rows.reshape(group_size, capacity, SEG, D),
        "fsdp",
        split_axis=0,
        concat_axis=0,
        tiled=True,
    )
    picked = jnp.take(received.reshape(group_size * capacity, SEG, D), row_index, axis=0)
    frames = jnp.where(is_live[:, None, None], picked, zero_bf).reshape(OWN_SEG * SEG, D)
    tap_terms = stem_taps(frames, stem_gathered)
    shifted = jnp.concatenate(
        [tap_terms[0][1:], jnp.zeros((1, tap_terms[0].shape[1]), jnp.float32)], 0
    )
    odd_rows = tap_terms[2] + shifted
    stem_rows = (
        jnp.concatenate([tap_terms[1], odd_rows], 1)
        .astype(jnp.bfloat16)
        .reshape(2 * OWN_SEG * SEG, tap_terms[0].shape[1])
    )
    shard_sum = y_site_sum(z_total).transpose(1, 0, 2).reshape(rows_out, D)
    weight_grad = shard_sum / math.sqrt(lax.axis_size("site") * group_size * HOLD * SEG)
    return (stem_rows[None], weight_grad)


def solution(mesh):
    placed = (
        P("site", "fsdp", None),
        P("site", "fsdp", None),
        P("fsdp", None),
        P(None, "fsdp", None),
        P("site", None),
    )
    return jax.shard_map(
        body,
        mesh=mesh,
        in_specs=placed,
        out_specs=(P("site", "fsdp", None), P("fsdp", None)),
        check_vma=False,
    )
```

```python
import functools
import math

import jax
import jax.numpy as jnp
from jax import lax
from jax.experimental import pallas as pl
from jax.experimental.pallas import tpu as pltpu
from jax.sharding import PartitionSpec as P

D = 1536
SEG = 8
HOLD = 64
OWN_SEG = 128
N_Z = 8


EPSILON = 1e-05


def stem_taps(frames, stem_gathered):
    devices, taps_n, chans = stem_gathered.shape[:3]
    width = devices * chans
    weights = stem_gathered.transpose(1, 0, 2, 3).reshape(taps_n * width, D)
    flat = lax.dot_general(frames, weights, (((1,), (1,)), ((), ())), preferred_element_type=jnp.float32)
    return [flat[:, tap * width:(tap + 1) * width] for tap in range(taps_n)]


def ring_pass(n, lanes, prepare=None):
    mesh_kind = pl.DeviceIdType.MESH
    for step in range(n):
        slot, prev = step % 2, (step + 1) % 2
        sources = []
        for lane_index, lane in enumerate(lanes):
            left, right, chunk_of, land, recv_buf, send_buf, recv_sems, send_sems, free_sem = lane
            if prepare is not None:
                prepare(lane_index, step)
            if step == 0:
                sources.append(chunk_of(step))
                continue
            pltpu.make_async_remote_copy(
                src_ref=send_buf.at[prev],
                dst_ref=recv_buf.at[prev],
                send_sem=send_sems.at[prev],
                recv_sem=recv_sems.at[prev],
                device_id=left,
                device_id_type=mesh_kind,
            ).wait_recv()
            target = land if step == n - 1 else send_buf.at[slot]
            target[...] = recv_buf[prev] + chunk_of(step)[...]
            if step <= n - 3:
                pl.semaphore_signal(free_sem, inc=1, device_id=left, device_id_type=mesh_kind)
            sources.append(send_buf.at[slot])
        if step == n - 1:
            break
        copies = []
        for lane, source in zip(lanes, sources):
            left, right, chunk_of, land, recv_buf, send_buf, recv_sems, send_sems, free_sem = lane
            if step >= 2:
                pl.semaphore_wait(free_sem, 1)
            copy = pltpu.make_async_remote_copy(
                src_ref=source,
                dst_ref=recv_buf.at[slot],
                send_sem=send_sems.at[slot],
                recv_sem=recv_sems.at[slot],
                device_id=right,
                device_id_type=mesh_kind,
            )
            copy.start()
            copies.append(copy)
        for copy in copies:
            copy.wait_send()


def z_sum_kernel(n_z, n_y, lo_ref, hi_ref, ztot, xbuf, zrecv, zsend, swap_sems, dsems, free_sems):
    me = lax.axis_index("fsdp")
    site = lax.axis_index("site")
    core = lax.rem(me, 2)
    chip = me // 2
    zc, yc = chip // n_y, lax.rem(chip, n_y)
    sibling = me + 1 - 2 * core

    def device(z):
        return (site, 2 * (lax.rem(z + n_z, n_z) * n_y + yc) + core)

    mesh_kind = pl.DeviceIdType.MESH
    barrier = pltpu.get_barrier_semaphore()
    peers = ((site, sibling), device(zc - 1), device(zc + 1))
    for peer in peers:
        pl.semaphore_signal(barrier, inc=1, device_id=peer, device_id_type=mesh_kind)
    pl.semaphore_wait(barrier, len(peers))
    ways = (1, -1)
    parts = (lo_ref, hi_ref)

    def rows(lane, step):
        column = lax.rem(zc - ways[lane] * (1 + step) + 2 * n_z, n_z)
        return pl.ds(column * n_y, n_y)

    def swap(lane, step):
        return pltpu.make_async_remote_copy(
            src_ref=parts[lane].at[1 - core, rows(lane, step)],
            dst_ref=xbuf.at[rows(lane, step), lane],
            send_sem=swap_sems.at[lane, step, 0],
            recv_sem=swap_sems.at[lane, step, 1],
            device_id=(site, sibling),
            device_id_type=mesh_kind,
        )

    for step in range(n_z):
        for lane in range(2):
            swap(lane, step).start()

    def prepare(lane, step):
        swap(lane, step).wait_recv()
        here = rows(lane, step)
        xbuf[here, lane] = xbuf[here, lane] + parts[lane][core, here]

    lanes = []
    for lane, way in enumerate(ways):

        def z_chunk(step, lane=lane):
            return xbuf.at[rows(lane, step), lane]

        lanes.append((
            device(zc - way), device(zc + way), z_chunk, ztot.at[:, lane],
            zrecv.at[lane], zsend.at[lane], dsems.at[lane, 0], dsems.at[lane, 1], free_sems.at[lane],
        ))
    ring_pass(n_z, lanes, prepare)
    for step in range(n_z):
        for lane in range(2):
            swap(lane, step).wait_send()


def y_site_kernel(n_y, n_site, ztot, out_ref, yrecv, ysend, ytot, slots, dsems, free_sems, site_send, site_recv):
    me = lax.axis_index("fsdp")
    site = lax.axis_index("site")
    core = lax.rem(me, 2)
    chip = me // 2
    zc, yc = chip // n_y, lax.rem(chip, n_y)

    def device(y):
        return (site, 2 * (zc * n_y + lax.rem(y + n_y, n_y)) + core)

    mesh_kind = pl.DeviceIdType.MESH
    barrier = pltpu.get_barrier_semaphore()
    peers = [device(yc - 1), device(yc + 1)]
    for step in range(1, n_site):
        peers.append((lax.rem(site + step, n_site), me))
    for peer in peers:
        pl.semaphore_signal(barrier, inc=1, device_id=peer, device_id_type=mesh_kind)
    pl.semaphore_wait(barrier, len(peers))
    lanes = []
    for lane, way in enumerate((1, -1)):

        def y_chunk(step, lane=lane, way=way):
            return ztot.at[lax.rem(yc - way * (1 + step) + 2 * n_y, n_y), lane]

        lanes.append((
            device(yc - way), device(yc + way), y_chunk, ytot.at[lane],
            yrecv.at[lane], ysend.at[lane], dsems.at[lane, 0], dsems.at[lane, 1], free_sems.at[lane],
        ))
    ring_pass(n_y, lanes)
    copies = []
    for step in range(1, n_site):
        peer = lax.rem(site + step, n_site)
        copy = pltpu.make_async_remote_copy(
            src_ref=ytot,
            dst_ref=slots.at[site],
            send_sem=site_send.at[step],
            recv_sem=site_recv.at[site],
            device_id=(peer, me),
            device_id_type=mesh_kind,
        )
        copy.start()
        copies.append(copy)
    slots[site] = ytot[...]
    for copy in copies:
        copy.wait_send()
    for step in range(1, n_site):
        src = lax.rem(site + step, n_site)
        pltpu.make_async_remote_copy(
            src_ref=ytot,
            dst_ref=slots.at[src],
            send_sem=site_send.at[0],
            recv_sem=site_recv.at[src],
            device_id=(src, me),
            device_id_type=mesh_kind,
        ).wait_recv()
    total = slots[0]
    for index in range(1, n_site):
        total = total + slots[index]
    out_ref[...] = total


def z_sum(lo, hi, n_z):
    n_chip = lo.shape[1]
    n_y = n_chip // n_z
    lane_block = lo.shape[2:]
    block = (2,) + lane_block
    return pl.pallas_call(
        functools.partial(z_sum_kernel, n_z, n_y),
        out_shape=jax.ShapeDtypeStruct((n_y,) + block, lo.dtype),
        in_specs=[pl.BlockSpec(memory_space=pltpu.VMEM)] * 2,
        out_specs=pl.BlockSpec(memory_space=pltpu.VMEM),
        scratch_shapes=[
            pltpu.VMEM((n_chip,) + block, lo.dtype),
            pltpu.VMEM((2, 2, n_y) + lane_block, lo.dtype),
            pltpu.VMEM((2, 2, n_y) + lane_block, lo.dtype),
            pltpu.SemaphoreType.DMA((2, n_z, 2)),
            pltpu.SemaphoreType.DMA((2, 2, 2)),
            pltpu.SemaphoreType.REGULAR((2,)),
        ],
        compiler_params=pltpu.CompilerParams(collective_id=1, has_side_effects=True),
    )(lo, hi)


def y_site_sum(ztot):
    n_y = ztot.shape[0]
    n_site = lax.axis_size("site")
    block = ztot.shape[1:]
    lane_block = ztot.shape[2:]
    return pl.pallas_call(
        functools.partial(y_site_kernel, n_y, n_site),
        out_shape=jax.ShapeDtypeStruct(block, ztot.dtype),
        in_specs=[pl.BlockSpec(memory_space=pltpu.VMEM)],
        out_specs=pl.BlockSpec(memory_space=pltpu.VMEM),
        scratch_shapes=[
            pltpu.VMEM((2, 2) + lane_block, ztot.dtype),
            pltpu.VMEM((2, 2) + lane_block, ztot.dtype),
            pltpu.VMEM(block, ztot.dtype),
            pltpu.VMEM((n_site,) + block, ztot.dtype),
            pltpu.SemaphoreType.DMA((2, 2, 2)),
            pltpu.SemaphoreType.REGULAR((2,)),
            pltpu.SemaphoreType.DMA((n_site,)),
            pltpu.SemaphoreType.DMA((n_site,)),
        ],
        compiler_params=pltpu.CompilerParams(collective_id=2, has_side_effects=True),
    )(ztot)


def body(held_input, held_cotangent, proj_weight, stem_weight, seg_counts):
    group_size = lax.axis_size("fsdp")
    capacity = 2 * ((OWN_SEG + 2 * group_size - 1) // (2 * group_size))
    my_index = lax.axis_index("fsdp")
    inputs = held_input[0].astype(jnp.float32)
    cotangent = held_cotangent[0]
    row_mean = jnp.mean(inputs, axis=-1, keepdims=True)
    centered = inputs - row_mean
    variance = jnp.mean(centered * centered, axis=-1, keepdims=True)
    inverse = lax.rsqrt(variance + EPSILON)
    normed = centered * inverse
    normed_bf = normed.astype(jnp.bfloat16)
    rows_w = proj_weight.shape[0]
    taps_n, chans = stem_weight.shape[0], stem_weight.shape[1]
    joined = jnp.concatenate([proj_weight, stem_weight.reshape(taps_n * chans, D)], 1)
    gathered = lax.all_gather(joined, "fsdp", axis=0, tiled=True)
    rows_out = D // group_size
    by_core = normed_bf.reshape(normed_bf.shape[0], group_size // 2, 2, rows_out)
    halves = [
        jnp.einsum("rckj,rd->kcjd", by_core, cotangent[:, part * (D // 2):(part + 1) * (D // 2)],
                   preferred_element_type=jnp.float32)
        for part in range(2)
    ]
    z_total = z_sum(halves[0], halves[1], N_Z)
    z_total, gathered = lax.optimization_barrier((z_total, gathered))
    full_weight = gathered[:, :D]
    stem_gathered = gathered[:, D:].reshape(group_size, taps_n, chans, D)
    proj_back = lax.dot_general(
        cotangent,
        full_weight,
        (((1,), (1,)), ((), ())),
        preferred_element_type=jnp.float32,
    )
    input_grad = cotangent.astype(jnp.float32) + inverse * (
        proj_back
        - jnp.mean(proj_back, axis=-1, keepdims=True)
        - normed * jnp.mean(proj_back * normed, axis=-1, keepdims=True)
    )
    input_grad = input_grad.astype(jnp.bfloat16)
    counts = seg_counts[0]
    endings = jnp.cumsum(counts)
    starts = endings - counts
    slot_ids = jnp.arange(HOLD, dtype=jnp.int32)
    item_index = 2 * (slot_ids // 2 * group_size + my_index) + slot_ids % 2
    owner_ids = jnp.sum((item_index[:, None] >= endings[None, :]).astype(jnp.int32), axis=1)
    earlier = (slot_ids[None, :] < slot_ids[:, None]) & (owner_ids[None, :] == owner_ids[:, None])
    rank_ids = jnp.sum(earlier.astype(jnp.int32), axis=1)
    target = owner_ids * capacity + rank_ids
    positions = jnp.arange(group_size * capacity, dtype=jnp.int32)
    matched = target[None, :] == positions[:, None]
    filled = jnp.any(matched, axis=1)
    source = jnp.sum(jnp.where(matched, slot_ids[None, :], 0), axis=1)
    owner_hit = jnp.arange(group_size, dtype=jnp.int32) == my_index
    my_count = jnp.sum(jnp.where(owner_hit, counts, 0))
    my_start = jnp.sum(jnp.where(owner_hit, starts, 0))
    segment = jnp.arange(OWN_SEG, dtype=jnp.int32)
    is_live = segment < my_count
    holder = (my_start + segment) // 2 % group_size
    before = (
        (segment[None, :] < segment[:, None])
        & (holder[None, :] == holder[:, None])
        & is_live[None, :]
    )
    holder_rank = jnp.sum(before.astype(jnp.int32), axis=1)
    row_index = jnp.where(is_live, holder * capacity + holder_rank, 0)
    held_segments = input_grad.reshape(HOLD, SEG, D)
    zero_bf = jnp.zeros((), jnp.bfloat16)
    send_rows = jnp.take(held_segments, source, axis=0, mode="clip")
    received = lax.all_to_all(
        send_rows.reshape(group_size, capacity, SEG, D),
        "fsdp",
        split_axis=0,
        concat_axis=0,
        tiled=True,
    )
    picked = jnp.take(received.reshape(group_size * capacity, SEG, D), row_index, axis=0, mode="clip")
    frames = jnp.where(is_live[:, None, None], picked, zero_bf).reshape(OWN_SEG * SEG, D)
    tap_terms = stem_taps(frames, stem_gathered)
    shifted = jnp.concatenate(
        [tap_terms[0][1:], jnp.zeros((1, tap_terms[0].shape[1]), jnp.float32)], 0
    )
    odd_rows = tap_terms[2] + shifted
    stem_rows = (
        jnp.concatenate([tap_terms[1], odd_rows], 1)
        .astype(jnp.bfloat16)
        .reshape(2 * OWN_SEG * SEG, tap_terms[0].shape[1])
    )
    shard_sum = y_site_sum(z_total).transpose(1, 0, 2).reshape(rows_out, D)
    weight_grad = shard_sum / math.sqrt(lax.axis_size("site") * group_size * HOLD * SEG)
    return (stem_rows[None], weight_grad)


def solution(mesh):
    placed = (
        P("site", "fsdp", None),
        P("site", "fsdp", None),
        P("fsdp", None),
        P(None, "fsdp", None),
        P("site", None),
    )
    return jax.shard_map(
        body,
        mesh=mesh,
        in_specs=placed,
        out_specs=(P("site", "fsdp", None), P("fsdp", None)),
        check_vma=False,
    )
```

```python
import functools
import math

import jax
import jax.numpy as jnp
from jax import lax
from jax.experimental import pallas as pl
from jax.experimental.pallas import tpu as pltpu
from jax.sharding import PartitionSpec as P

D = 1536
SEG = 8
HOLD = 64
OWN_SEG = 128
N_Z = 8


EPSILON = 1e-05


def stem_taps(frames, stem_gathered):
    devices, taps_n, chans = stem_gathered.shape[:3]
    width = devices * chans
    weights = stem_gathered.transpose(1, 0, 2, 3).reshape(taps_n * width, D)
    flat = lax.dot_general(frames, weights, (((1,), (1,)), ((), ())), preferred_element_type=jnp.float32)
    return [flat[:, tap * width:(tap + 1) * width] for tap in range(taps_n)]


def ring_pass(n, lanes, prepare=None):
    mesh_kind = pl.DeviceIdType.MESH
    for step in range(n):
        slot, prev = step % 2, (step + 1) % 2
        sources = []
        for lane_index, lane in enumerate(lanes):
            left, right, chunk_of, land, recv_buf, send_buf, recv_sems, send_sems, free_sem = lane
            if prepare is not None:
                prepare(lane_index, step)
            if step == 0:
                sources.append(chunk_of(step))
                continue
            pltpu.make_async_remote_copy(
                src_ref=send_buf.at[prev],
                dst_ref=recv_buf.at[prev],
                send_sem=send_sems.at[prev],
                recv_sem=recv_sems.at[prev],
                device_id=left,
                device_id_type=mesh_kind,
            ).wait_recv()
            target = land if step == n - 1 else send_buf.at[slot]
            target[...] = recv_buf[prev] + chunk_of(step)[...]
            if step <= n - 3:
                pl.semaphore_signal(free_sem, inc=1, device_id=left, device_id_type=mesh_kind)
            sources.append(send_buf.at[slot])
        if step == n - 1:
            break
        copies = []
        for lane, source in zip(lanes, sources):
            left, right, chunk_of, land, recv_buf, send_buf, recv_sems, send_sems, free_sem = lane
            if step >= 2:
                pl.semaphore_wait(free_sem, 1)
            copy = pltpu.make_async_remote_copy(
                src_ref=source,
                dst_ref=recv_buf.at[slot],
                send_sem=send_sems.at[slot],
                recv_sem=recv_sems.at[slot],
                device_id=right,
                device_id_type=mesh_kind,
            )
            copy.start()
            copies.append(copy)
        for copy in copies:
            copy.wait_send()


def z_sum_kernel(n_z, n_y, lo_ref, hi_ref, ztot, xbuf, zrecv, zsend, swap_sems, dsems, free_sems):
    me = lax.axis_index("fsdp")
    site = lax.axis_index("site")
    core = lax.rem(me, 2)
    chip = me // 2
    zc, yc = chip // n_y, lax.rem(chip, n_y)
    sibling = me + 1 - 2 * core

    def device(z):
        return (site, 2 * (lax.rem(z + n_z, n_z) * n_y + yc) + core)

    mesh_kind = pl.DeviceIdType.MESH
    barrier = pltpu.get_barrier_semaphore()
    peers = ((site, sibling), device(zc - 1), device(zc + 1))
    for peer in peers:
        pl.semaphore_signal(barrier, inc=1, device_id=peer, device_id_type=mesh_kind)
    pl.semaphore_wait(barrier, len(peers))
    ways = (1, -1)
    parts = (lo_ref, hi_ref)

    def rows(lane, step):
        column = lax.rem(zc - ways[lane] * (1 + step) + 2 * n_z, n_z)
        return pl.ds(column * n_y, n_y)

    def swap(lane, step):
        return pltpu.make_async_remote_copy(
            src_ref=parts[lane].at[1 - core, rows(lane, step)],
            dst_ref=xbuf.at[rows(lane, step), lane],
            send_sem=swap_sems.at[lane, step, 0],
            recv_sem=swap_sems.at[lane, step, 1],
            device_id=(site, sibling),
            device_id_type=mesh_kind,
        )

    for step in range(n_z):
        for lane in range(2):
            swap(lane, step).start()

    def prepare(lane, step):
        swap(lane, step).wait_recv()
        here = rows(lane, step)
        xbuf[here, lane] = xbuf[here, lane] + parts[lane][core, here]

    lanes = []
    for lane, way in enumerate(ways):

        def z_chunk(step, lane=lane):
            return xbuf.at[rows(lane, step), lane]

        lanes.append((
            device(zc - way), device(zc + way), z_chunk, ztot.at[:, lane],
            zrecv.at[lane], zsend.at[lane], dsems.at[lane, 0], dsems.at[lane, 1], free_sems.at[lane],
        ))
    ring_pass(n_z, lanes, prepare)
    for step in range(n_z):
        for lane in range(2):
            swap(lane, step).wait_send()


def y_site_kernel(n_y, n_site, ztot, out_ref, yrecv, ysend, ytot, slots, dsems, free_sems, site_send, site_recv):
    me = lax.axis_index("fsdp")
    site = lax.axis_index("site")
    core = lax.rem(me, 2)
    chip = me // 2
    zc, yc = chip // n_y, lax.rem(chip, n_y)

    def device(y):
        return (site, 2 * (zc * n_y + lax.rem(y + n_y, n_y)) + core)

    mesh_kind = pl.DeviceIdType.MESH
    barrier = pltpu.get_barrier_semaphore()
    peers = [device(yc - 1), device(yc + 1)]
    for step in range(1, n_site):
        peers.append((lax.rem(site + step, n_site), me))
    for peer in peers:
        pl.semaphore_signal(barrier, inc=1, device_id=peer, device_id_type=mesh_kind)
    pl.semaphore_wait(barrier, len(peers))
    lanes = []
    for lane, way in enumerate((1, -1)):

        def y_chunk(step, lane=lane, way=way):
            return ztot.at[lax.rem(yc - way * (1 + step) + 2 * n_y, n_y), lane]

        lanes.append((
            device(yc - way), device(yc + way), y_chunk, ytot.at[lane],
            yrecv.at[lane], ysend.at[lane], dsems.at[lane, 0], dsems.at[lane, 1], free_sems.at[lane],
        ))
    ring_pass(n_y, lanes)
    copies = []
    for step in range(1, n_site):
        peer = lax.rem(site + step, n_site)
        copy = pltpu.make_async_remote_copy(
            src_ref=ytot,
            dst_ref=slots.at[site],
            send_sem=site_send.at[step],
            recv_sem=site_recv.at[site],
            device_id=(peer, me),
            device_id_type=mesh_kind,
        )
        copy.start()
        copies.append(copy)
    slots[site] = ytot[...]
    for copy in copies:
        copy.wait_send()
    for step in range(1, n_site):
        src = lax.rem(site + step, n_site)
        pltpu.make_async_remote_copy(
            src_ref=ytot,
            dst_ref=slots.at[src],
            send_sem=site_send.at[0],
            recv_sem=site_recv.at[src],
            device_id=(src, me),
            device_id_type=mesh_kind,
        ).wait_recv()
    total = slots[0]
    for index in range(1, n_site):
        total = total + slots[index]
    out_ref[...] = total


def z_sum(lo, hi, n_z):
    n_chip = lo.shape[1]
    n_y = n_chip // n_z
    lane_block = lo.shape[2:]
    block = (2,) + lane_block
    return pl.pallas_call(
        functools.partial(z_sum_kernel, n_z, n_y),
        out_shape=jax.ShapeDtypeStruct((n_y,) + block, lo.dtype),
        in_specs=[pl.BlockSpec(memory_space=pltpu.VMEM)] * 2,
        out_specs=pl.BlockSpec(memory_space=pltpu.VMEM),
        scratch_shapes=[
            pltpu.VMEM((n_chip,) + block, lo.dtype),
            pltpu.VMEM((2, 2, n_y) + lane_block, lo.dtype),
            pltpu.VMEM((2, 2, n_y) + lane_block, lo.dtype),
            pltpu.SemaphoreType.DMA((2, n_z, 2)),
            pltpu.SemaphoreType.DMA((2, 2, 2)),
            pltpu.SemaphoreType.REGULAR((2,)),
        ],
        compiler_params=pltpu.CompilerParams(collective_id=1, has_side_effects=True),
    )(lo, hi)


def y_site_sum(ztot):
    n_y = ztot.shape[0]
    n_site = lax.axis_size("site")
    block = ztot.shape[1:]
    lane_block = ztot.shape[2:]
    return pl.pallas_call(
        functools.partial(y_site_kernel, n_y, n_site),
        out_shape=jax.ShapeDtypeStruct(block, ztot.dtype),
        in_specs=[pl.BlockSpec(memory_space=pltpu.VMEM)],
        out_specs=pl.BlockSpec(memory_space=pltpu.VMEM),
        scratch_shapes=[
            pltpu.VMEM((2, 2) + lane_block, ztot.dtype),
            pltpu.VMEM((2, 2) + lane_block, ztot.dtype),
            pltpu.VMEM(block, ztot.dtype),
            pltpu.VMEM((n_site,) + block, ztot.dtype),
            pltpu.SemaphoreType.DMA((2, 2, 2)),
            pltpu.SemaphoreType.REGULAR((2,)),
            pltpu.SemaphoreType.DMA((n_site,)),
            pltpu.SemaphoreType.DMA((n_site,)),
        ],
        compiler_params=pltpu.CompilerParams(collective_id=2, has_side_effects=True),
    )(ztot)


def body(held_input, held_cotangent, proj_weight, stem_weight, seg_counts):
    group_size = lax.axis_size("fsdp")
    capacity = 2 * ((OWN_SEG + 2 * group_size - 1) // (2 * group_size))
    my_index = lax.axis_index("fsdp")
    inputs = held_input[0].astype(jnp.float32)
    cotangent = held_cotangent[0]
    row_mean = jnp.mean(inputs, axis=-1, keepdims=True)
    centered = inputs - row_mean
    variance = jnp.mean(centered * centered, axis=-1, keepdims=True)
    inverse = lax.rsqrt(variance + EPSILON)
    normed = centered * inverse
    normed_bf = normed.astype(jnp.bfloat16)
    rows_w = proj_weight.shape[0]
    taps_n, chans = stem_weight.shape[0], stem_weight.shape[1]
    joined = jnp.concatenate([proj_weight, stem_weight.reshape(taps_n * chans, D)], 1)
    gathered = lax.all_gather(joined, "fsdp", axis=0, tiled=True)
    rows_out = D // group_size
    by_core = normed_bf.reshape(normed_bf.shape[0], group_size // 2, 2, rows_out)
    halves = [
        jnp.einsum("rckj,rd->kcjd", by_core, cotangent[:, part * (D // 2):(part + 1) * (D // 2)],
                   preferred_element_type=jnp.float32)
        for part in range(2)
    ]
    z_total = z_sum(halves[0], halves[1], N_Z)
    z_total, gathered = lax.optimization_barrier((z_total, gathered))
    full_weight = gathered[:, :D]
    stem_gathered = gathered[:, D:].reshape(group_size, taps_n, chans, D)
    proj_back = lax.dot_general(
        cotangent,
        full_weight,
        (((1,), (1,)), ((), ())),
        preferred_element_type=jnp.float32,
    )
    sum_back, sum_cross = lax.reduce(
        (proj_back, proj_back * normed),
        (jnp.float32(0), jnp.float32(0)),
        lambda a, b: (a[0] + b[0], a[1] + b[1]),
        (1,),
    )
    input_grad = cotangent.astype(jnp.float32) + inverse * (
        proj_back - (sum_back / D)[:, None] - normed * (sum_cross / D)[:, None]
    )
    input_grad = input_grad.astype(jnp.bfloat16)
    counts = seg_counts[0]
    endings = jnp.cumsum(counts)
    starts = endings - counts
    slot_ids = jnp.arange(HOLD, dtype=jnp.int32)
    item_index = 2 * (slot_ids // 2 * group_size + my_index) + slot_ids % 2
    owner_ids = jnp.sum((item_index[:, None] >= endings[None, :]).astype(jnp.int32), axis=1)
    earlier = (slot_ids[None, :] < slot_ids[:, None]) & (owner_ids[None, :] == owner_ids[:, None])
    rank_ids = jnp.sum(earlier.astype(jnp.int32), axis=1)
    target = owner_ids * capacity + rank_ids
    positions = jnp.arange(group_size * capacity, dtype=jnp.int32)
    matched = target[None, :] == positions[:, None]
    filled = jnp.any(matched, axis=1)
    source = jnp.sum(jnp.where(matched, slot_ids[None, :], 0), axis=1)
    owner_hit = jnp.arange(group_size, dtype=jnp.int32) == my_index
    my_count = jnp.sum(jnp.where(owner_hit, counts, 0))
    my_start = jnp.sum(jnp.where(owner_hit, starts, 0))
    segment = jnp.arange(OWN_SEG, dtype=jnp.int32)
    is_live = segment < my_count
    holder = (my_start + segment) // 2 % group_size
    before = (
        (segment[None, :] < segment[:, None])
        & (holder[None, :] == holder[:, None])
        & is_live[None, :]
    )
    holder_rank = jnp.sum(before.astype(jnp.int32), axis=1)
    row_index = jnp.where(is_live, holder * capacity + holder_rank, 0)
    held_segments = input_grad.reshape(HOLD, SEG, D)
    zero_bf = jnp.zeros((), jnp.bfloat16)
    send_rows = jnp.take(held_segments, source, axis=0, mode="clip")
    received = lax.all_to_all(
        send_rows.reshape(group_size, capacity, SEG, D),
        "fsdp",
        split_axis=0,
        concat_axis=0,
        tiled=True,
    )
    picked = jnp.take(received.reshape(group_size * capacity, SEG, D), row_index, axis=0, mode="clip")
    frames = jnp.where(is_live[:, None, None], picked, zero_bf).reshape(OWN_SEG * SEG, D)
    tap_terms = stem_taps(frames, stem_gathered)
    shifted = jnp.concatenate(
        [tap_terms[0][1:], jnp.zeros((1, tap_terms[0].shape[1]), jnp.float32)], 0
    )
    odd_rows = tap_terms[2] + shifted
    stem_rows = (
        jnp.concatenate([tap_terms[1], odd_rows], 1)
        .astype(jnp.bfloat16)
        .reshape(2 * OWN_SEG * SEG, tap_terms[0].shape[1])
    )
    shard_sum = y_site_sum(z_total).transpose(1, 0, 2).reshape(rows_out, D)
    weight_grad = shard_sum / math.sqrt(lax.axis_size("site") * group_size * HOLD * SEG)
    return (stem_rows[None], weight_grad)


def solution(mesh):
    placed = (
        P("site", "fsdp", None),
        P("site", "fsdp", None),
        P("fsdp", None),
        P(None, "fsdp", None),
        P("site", None),
    )
    return jax.shard_map(
        body,
        mesh=mesh,
        in_specs=placed,
        out_specs=(P("site", "fsdp", None), P("fsdp", None)),
        check_vma=False,
    )
```

```python
import functools
import math

import jax
import jax.numpy as jnp
from jax import lax
from jax.experimental import pallas as pl
from jax.experimental.pallas import tpu as pltpu
from jax.sharding import PartitionSpec as P

D = 1536
SEG = 8
HOLD = 64
OWN_SEG = 128
N_Z = 8


EPSILON = 1e-05


def stem_taps(frames, stem_gathered):
    devices, taps_n, chans = stem_gathered.shape[:3]
    width = devices * chans
    weights = stem_gathered.transpose(1, 0, 2, 3).reshape(taps_n * width, D)
    flat = lax.dot_general(frames, weights, (((1,), (1,)), ((), ())), preferred_element_type=jnp.float32)
    return [flat[:, tap * width:(tap + 1) * width] for tap in range(taps_n)]


def ring_pass(n, lanes, prepare=None):
    mesh_kind = pl.DeviceIdType.MESH
    for step in range(n):
        slot, prev = step % 2, (step + 1) % 2
        sources = []
        for lane_index, lane in enumerate(lanes):
            left, right, chunk_of, land, recv_buf, send_buf, recv_sems, send_sems, free_sem = lane
            if prepare is not None:
                prepare(lane_index, step)
            if step == 0:
                sources.append(chunk_of(step))
                continue
            pltpu.make_async_remote_copy(
                src_ref=send_buf.at[prev],
                dst_ref=recv_buf.at[prev],
                send_sem=send_sems.at[prev],
                recv_sem=recv_sems.at[prev],
                device_id=left,
                device_id_type=mesh_kind,
            ).wait_recv()
            target = land if step == n - 1 else send_buf.at[slot]
            target[...] = recv_buf[prev] + chunk_of(step)[...]
            if step <= n - 3:
                pl.semaphore_signal(free_sem, inc=1, device_id=left, device_id_type=mesh_kind)
            sources.append(send_buf.at[slot])
        if step == n - 1:
            break
        copies = []
        for lane, source in zip(lanes, sources):
            left, right, chunk_of, land, recv_buf, send_buf, recv_sems, send_sems, free_sem = lane
            if step >= 2:
                pl.semaphore_wait(free_sem, 1)
            copy = pltpu.make_async_remote_copy(
                src_ref=source,
                dst_ref=recv_buf.at[slot],
                send_sem=send_sems.at[slot],
                recv_sem=recv_sems.at[slot],
                device_id=right,
                device_id_type=mesh_kind,
            )
            copy.start()
            copies.append(copy)
        for copy in copies:
            copy.wait_send()


def z_sum_kernel(n_z, n_y, lo_ref, hi_ref, ztot, xbuf, zrecv, zsend, swap_sems, dsems, free_sems):
    me = lax.axis_index("fsdp")
    site = lax.axis_index("site")
    core = lax.rem(me, 2)
    chip = me // 2
    zc, yc = chip // n_y, lax.rem(chip, n_y)
    sibling = me + 1 - 2 * core

    def device(z):
        return (site, 2 * (lax.rem(z + n_z, n_z) * n_y + yc) + core)

    mesh_kind = pl.DeviceIdType.MESH
    barrier = pltpu.get_barrier_semaphore()
    peers = ((site, sibling), device(zc - 1), device(zc + 1))
    for peer in peers:
        pl.semaphore_signal(barrier, inc=1, device_id=peer, device_id_type=mesh_kind)
    pl.semaphore_wait(barrier, len(peers))
    ways = (1, -1)
    parts = (lo_ref, hi_ref)

    def rows(lane, step):
        column = lax.rem(zc - ways[lane] * (1 + step) + 2 * n_z, n_z)
        return pl.ds(column * n_y, n_y)

    def swap(lane, step):
        return pltpu.make_async_remote_copy(
            src_ref=parts[lane].at[1 - core, rows(lane, step)],
            dst_ref=xbuf.at[rows(lane, step), lane],
            send_sem=swap_sems.at[lane, step, 0],
            recv_sem=swap_sems.at[lane, step, 1],
            device_id=(site, sibling),
            device_id_type=mesh_kind,
        )

    for step in range(n_z):
        for lane in range(2):
            swap(lane, step).start()

    def prepare(lane, step):
        swap(lane, step).wait_recv()
        here = rows(lane, step)
        xbuf[here, lane] = xbuf[here, lane] + parts[lane][core, here]

    lanes = []
    for lane, way in enumerate(ways):

        def z_chunk(step, lane=lane):
            return xbuf.at[rows(lane, step), lane]

        lanes.append((
            device(zc - way), device(zc + way), z_chunk, ztot.at[:, lane],
            zrecv.at[lane], zsend.at[lane], dsems.at[lane, 0], dsems.at[lane, 1], free_sems.at[lane],
        ))
    ring_pass(n_z, lanes, prepare)
    for step in range(n_z):
        for lane in range(2):
            swap(lane, step).wait_send()


def y_site_kernel(n_y, n_site, ztot, out_ref, yrecv, ysend, ytot, slots, dsems, free_sems, site_send, site_recv):
    me = lax.axis_index("fsdp")
    site = lax.axis_index("site")
    core = lax.rem(me, 2)
    chip = me // 2
    zc, yc = chip // n_y, lax.rem(chip, n_y)

    def device(y):
        return (site, 2 * (zc * n_y + lax.rem(y + n_y, n_y)) + core)

    mesh_kind = pl.DeviceIdType.MESH
    barrier = pltpu.get_barrier_semaphore()
    peers = [device(yc - 1), device(yc + 1)]
    for step in range(1, n_site):
        peers.append((lax.rem(site + step, n_site), me))
    for peer in peers:
        pl.semaphore_signal(barrier, inc=1, device_id=peer, device_id_type=mesh_kind)
    pl.semaphore_wait(barrier, len(peers))
    lanes = []
    for lane, way in enumerate((1, -1)):

        def y_chunk(step, lane=lane, way=way):
            return ztot.at[lax.rem(yc - way * (1 + step) + 2 * n_y, n_y), lane]

        lanes.append((
            device(yc - way), device(yc + way), y_chunk, ytot.at[lane],
            yrecv.at[lane], ysend.at[lane], dsems.at[lane, 0], dsems.at[lane, 1], free_sems.at[lane],
        ))
    ring_pass(n_y, lanes)
    copies = []
    for step in range(1, n_site):
        peer = lax.rem(site + step, n_site)
        copy = pltpu.make_async_remote_copy(
            src_ref=ytot,
            dst_ref=slots.at[site],
            send_sem=site_send.at[step],
            recv_sem=site_recv.at[site],
            device_id=(peer, me),
            device_id_type=mesh_kind,
        )
        copy.start()
        copies.append(copy)
    slots[site] = ytot[...]
    for copy in copies:
        copy.wait_send()
    for step in range(1, n_site):
        src = lax.rem(site + step, n_site)
        pltpu.make_async_remote_copy(
            src_ref=ytot,
            dst_ref=slots.at[src],
            send_sem=site_send.at[0],
            recv_sem=site_recv.at[src],
            device_id=(src, me),
            device_id_type=mesh_kind,
        ).wait_recv()
    total = slots[0]
    for index in range(1, n_site):
        total = total + slots[index]
    out_ref[...] = total


def z_sum(lo, hi, n_z):
    n_chip = lo.shape[1]
    n_y = n_chip // n_z
    lane_block = lo.shape[2:]
    block = (2,) + lane_block
    return pl.pallas_call(
        functools.partial(z_sum_kernel, n_z, n_y),
        out_shape=jax.ShapeDtypeStruct((n_y,) + block, lo.dtype),
        in_specs=[pl.BlockSpec(memory_space=pltpu.VMEM)] * 2,
        out_specs=pl.BlockSpec(memory_space=pltpu.VMEM),
        scratch_shapes=[
            pltpu.VMEM((n_chip,) + block, lo.dtype),
            pltpu.VMEM((2, 2, n_y) + lane_block, lo.dtype),
            pltpu.VMEM((2, 2, n_y) + lane_block, lo.dtype),
            pltpu.SemaphoreType.DMA((2, n_z, 2)),
            pltpu.SemaphoreType.DMA((2, 2, 2)),
            pltpu.SemaphoreType.REGULAR((2,)),
        ],
        compiler_params=pltpu.CompilerParams(collective_id=1, has_side_effects=True),
    )(lo, hi)


def y_site_sum(ztot):
    n_y = ztot.shape[0]
    n_site = lax.axis_size("site")
    block = ztot.shape[1:]
    lane_block = ztot.shape[2:]
    return pl.pallas_call(
        functools.partial(y_site_kernel, n_y, n_site),
        out_shape=jax.ShapeDtypeStruct(block, ztot.dtype),
        in_specs=[pl.BlockSpec(memory_space=pltpu.VMEM)],
        out_specs=pl.BlockSpec(memory_space=pltpu.VMEM),
        scratch_shapes=[
            pltpu.VMEM((2, 2) + lane_block, ztot.dtype),
            pltpu.VMEM((2, 2) + lane_block, ztot.dtype),
            pltpu.VMEM(block, ztot.dtype),
            pltpu.VMEM((n_site,) + block, ztot.dtype),
            pltpu.SemaphoreType.DMA((2, 2, 2)),
            pltpu.SemaphoreType.REGULAR((2,)),
            pltpu.SemaphoreType.DMA((n_site,)),
            pltpu.SemaphoreType.DMA((n_site,)),
        ],
        compiler_params=pltpu.CompilerParams(collective_id=2, has_side_effects=True),
    )(ztot)


def body(held_input, held_cotangent, proj_weight, stem_weight, seg_counts):
    group_size = lax.axis_size("fsdp")
    capacity = 2 * ((OWN_SEG + 2 * group_size - 1) // (2 * group_size))
    my_index = lax.axis_index("fsdp")
    inputs = held_input[0].astype(jnp.float32)
    cotangent = held_cotangent[0]
    row_mean = jnp.mean(inputs, axis=-1, keepdims=True)
    centered = inputs - row_mean
    variance = jnp.mean(centered * centered, axis=-1, keepdims=True)
    inverse = lax.rsqrt(variance + EPSILON)
    normed = centered * inverse
    normed_bf = normed.astype(jnp.bfloat16)
    rows_w = proj_weight.shape[0]
    taps_n, chans = stem_weight.shape[0], stem_weight.shape[1]
    joined = jnp.concatenate([proj_weight, stem_weight.reshape(taps_n * chans, D)], 1)
    gathered = lax.all_gather(joined, "fsdp", axis=0, tiled=True)
    rows_out = D // group_size
    by_core = normed_bf.T.reshape(group_size // 2, 2, rows_out, normed_bf.shape[0])
    halves = [
        jnp.einsum("ckjr,rd->kcjd", by_core, cotangent[:, part * (D // 2):(part + 1) * (D // 2)],
                   preferred_element_type=jnp.float32)
        for part in range(2)
    ]
    z_total = z_sum(halves[0], halves[1], N_Z)
    z_total, gathered = lax.optimization_barrier((z_total, gathered))
    full_weight = gathered[:, :D]
    stem_gathered = gathered[:, D:].reshape(group_size, taps_n, chans, D)
    proj_back = lax.dot_general(
        cotangent,
        full_weight,
        (((1,), (1,)), ((), ())),
        preferred_element_type=jnp.float32,
    )
    input_grad = cotangent.astype(jnp.float32) + inverse * (
        proj_back
        - jnp.mean(proj_back, axis=-1, keepdims=True)
        - normed * jnp.mean(proj_back * normed, axis=-1, keepdims=True)
    )
    input_grad = input_grad.astype(jnp.bfloat16)
    counts = seg_counts[0]
    endings = jnp.cumsum(counts)
    starts = endings - counts
    slot_ids = jnp.arange(HOLD, dtype=jnp.int32)
    item_index = 2 * (slot_ids // 2 * group_size + my_index) + slot_ids % 2
    owner_ids = jnp.sum((item_index[:, None] >= endings[None, :]).astype(jnp.int32), axis=1)
    earlier = (slot_ids[None, :] < slot_ids[:, None]) & (owner_ids[None, :] == owner_ids[:, None])
    rank_ids = jnp.sum(earlier.astype(jnp.int32), axis=1)
    target = owner_ids * capacity + rank_ids
    positions = jnp.arange(group_size * capacity, dtype=jnp.int32)
    matched = target[None, :] == positions[:, None]
    filled = jnp.any(matched, axis=1)
    source = jnp.sum(jnp.where(matched, slot_ids[None, :], 0), axis=1)
    owner_hit = jnp.arange(group_size, dtype=jnp.int32) == my_index
    my_count = jnp.sum(jnp.where(owner_hit, counts, 0))
    my_start = jnp.sum(jnp.where(owner_hit, starts, 0))
    segment = jnp.arange(OWN_SEG, dtype=jnp.int32)
    is_live = segment < my_count
    holder = (my_start + segment) // 2 % group_size
    before = (
        (segment[None, :] < segment[:, None])
        & (holder[None, :] == holder[:, None])
        & is_live[None, :]
    )
    holder_rank = jnp.sum(before.astype(jnp.int32), axis=1)
    row_index = jnp.where(is_live, holder * capacity + holder_rank, 0)
    held_segments = input_grad.reshape(HOLD, SEG, D)
    zero_bf = jnp.zeros((), jnp.bfloat16)
    send_rows = jnp.take(held_segments, source, axis=0, mode="clip")
    received = lax.all_to_all(
        send_rows.reshape(group_size, capacity, SEG, D),
        "fsdp",
        split_axis=0,
        concat_axis=0,
        tiled=True,
    )
    picked = jnp.take(received.reshape(group_size * capacity, SEG, D), row_index, axis=0, mode="clip")
    frames = jnp.where(is_live[:, None, None], picked, zero_bf).reshape(OWN_SEG * SEG, D)
    tap_terms = stem_taps(frames, stem_gathered)
    shifted = jnp.concatenate(
        [tap_terms[0][1:], jnp.zeros((1, tap_terms[0].shape[1]), jnp.float32)], 0
    )
    odd_rows = tap_terms[2] + shifted
    stem_rows = (
        jnp.concatenate([tap_terms[1], odd_rows], 1)
        .astype(jnp.bfloat16)
        .reshape(2 * OWN_SEG * SEG, tap_terms[0].shape[1])
    )
    shard_sum = y_site_sum(z_total).transpose(1, 0, 2).reshape(rows_out, D)
    weight_grad = shard_sum / math.sqrt(lax.axis_size("site") * group_size * HOLD * SEG)
    return (stem_rows[None], weight_grad)


def solution(mesh):
    placed = (
        P("site", "fsdp", None),
        P("site", "fsdp", None),
        P("fsdp", None),
        P(None, "fsdp", None),
        P("site", None),
    )
    return jax.shard_map(
        body,
        mesh=mesh,
        in_specs=placed,
        out_specs=(P("site", "fsdp", None), P("fsdp", None)),
        check_vma=False,
    )
```
